32 devices in a mesh: blk: 4 (over y, x), rep: 8 (over z, core).
Axes of the slice: x: 2, y: 2, z: 4, core: 2. Of those that a mesh axis runs over, the one named last changes fastest.
Arguments:
- image_feats: bfloat16 [8, 2048, 1024], P('rep', 'blk'), may hold values from -6 to 6
- text_feats: bfloat16 [8, 2048, 768], P('rep', 'blk'), may hold values from -6 to 6
- image_head: bfloat16 [1024, 768], replicated, may hold values from -0.1875 to 0.1875
- text_head: bfloat16 [768, 768], replicated, may hold values from -0.21875 to 0.21875
- image_lse: float32 [8, 2048], P('rep', 'blk'), as said below
- text_lse: float32 [8, 2048], P('rep', 'blk'), as said below
Outputs:
- image_feat_grad: float32 [8, 2048, 1024], P('rep', 'blk')
- text_feat_grad: float32 [8, 2048, 768], P('rep', 'blk')
- image_head_grad: float32 [1024, 768], replicated
- text_head_grad: float32 [768, 768], replicated
The draws below stay inside these ranges and needn't reach their ends.
Inputs may be any that keep to these rules, and one draw needn't show every extreme that they name: `image_lse`: each entry lies between ln(2048) + 1 and ln(2048) + 2.5. `text_lse`: each entry lies between ln(2048) + 1 and ln(2048) + 2.5.
All inputs are finite; a program needn't handle non-finite values.
Results may differ from the reference program's by a relative error of at most 0.028.
Values may be sent and summed in bfloat16 or wider, within the bound.
A program may use at most 128 MiB of HBM per device.

```python
import jax
import jax.numpy as jnp
from jax import lax

EMBED = 768
VIS_WIDTH = 1024
TXT_WIDTH = 768
PAIRS = 2048
GROUPS = 8


def normalizer_values(key, salt):
    base = jax.random.fold_in(key, salt)
    lowest = jnp.log(jnp.float32(PAIRS)) + 1.0
    pick = jax.random.uniform(jax.random.fold_in(base, 1), (GROUPS, PAIRS), jnp.float32)
    offset = 1.5 * pick
    return lowest + offset


def draw_image_lse(key, part):
    return normalizer_values(key, 11)


def draw_text_lse(key, part):
    return normalizer_values(key, 23)


def shard_levels(key, extent, cuts, least, largest):
    level, own = 1.0, jax.random.fold_in(key, 6)
    for dim, parts in cuts:
        heights = jnp.exp(jax.random.uniform(jax.random.fold_in(own, dim), (parts,), jnp.float32, least / len(cuts), largest / len(cuts)))
        level = level * jnp.repeat(heights, extent[dim] // parts).reshape([-1 if axis == dim else 1 for axis in range(len(extent))])
    return level


def normal_values(key, shape, scale, bound, pieces=(), held_as=jnp.bfloat16):
    result = jax.random.normal(key, shape, jnp.float32) * scale
    if len(pieces) > 0:
        result = shard_levels(key, shape, pieces, -0.22, 0.18) * result
    return jnp.clip(result, min=-bound, max=bound).astype(held_as)


def setup_inputs(seed: int = 0) -> dict:
    keys = jax.random.split(jax.random.key(seed), 7)
    return {
        "image_feats": normal_values(keys[0], (GROUPS, PAIRS, VIS_WIDTH), 1.0, 6.0, ((0, 8), (1, 4))),
        "text_feats": normal_values(keys[1], (GROUPS, PAIRS, TXT_WIDTH), 1.0, 6.0, ((0, 8), (1, 4))),
        "image_head": normal_values(keys[2], (VIS_WIDTH, EMBED), VIS_WIDTH ** -0.5, 0.1875),
        "text_head": normal_values(keys[3], (TXT_WIDTH, EMBED), TXT_WIDTH ** -0.5, 0.21875),
        "image_lse": draw_image_lse(jax.random.fold_in(keys[6], 71), 0),
        "text_lse": draw_text_lse(jax.random.fold_in(keys[6], 71), 0),
    }


logit_scale = 50.0
epsilon = 1e-06

def project_head(feats, weight):
    raw = jnp.dot(feats, weight, preferred_element_type=jnp.float32)
    factor = lax.rsqrt(lax.optimization_barrier(jnp.sum(raw * raw, axis=1, keepdims=True)) + epsilon)
    return (raw * factor, factor)

def pre_gradient(embed, factor, grad):
    inner = lax.optimization_barrier(jnp.sum(embed * grad, axis=1, keepdims=True))
    return (factor * (grad - embed * inner)).astype(jnp.bfloat16)

def group_grads(group):
    image_rows, text_rows, image_head, text_head, lse_img, lse_txt = group
    image_embed, image_scale = project_head(image_rows, image_head)
    text_embed, text_scale = project_head(text_rows, text_head)
    image_round = image_embed.astype(jnp.bfloat16)
    text_round = text_embed.astype(jnp.bfloat16)
    scores = logit_scale * lax.dot_general(image_round, text_round, (((1,), (1,)), ((), ())), preferred_element_type=jnp.float32)
    weights = (0.5 * (jnp.exp(scores - lse_img[:, None]) + jnp.exp(scores - lse_txt[None, :]))).astype(jnp.bfloat16)
    image_sum = jnp.dot(weights, text_round, preferred_element_type=jnp.float32)
    text_sum = lax.dot_general(weights, image_round, (((0,), (0,)), ((), ())), preferred_element_type=jnp.float32)
    image_grad = logit_scale * image_sum - logit_scale * text_round.astype(jnp.float32)
    text_grad = logit_scale * text_sum - logit_scale * image_round.astype(jnp.float32)
    image_pre = pre_gradient(image_embed, image_scale, image_grad)
    text_pre = pre_gradient(text_embed, text_scale, text_grad)
    image_back = lax.dot_general(image_pre, image_head, (((1,), (1,)), ((), ())), preferred_element_type=jnp.float32)
    text_back = lax.dot_general(text_pre, text_head, (((1,), (1,)), ((), ())), preferred_element_type=jnp.float32)
    image_wgrad = lax.dot_general(image_rows, image_pre, (((0,), (0,)), ((), ())), preferred_element_type=jnp.float32)
    text_wgrad = lax.dot_general(text_rows, text_pre, (((0,), (0,)), ((), ())), preferred_element_type=jnp.float32)
    return (image_back, text_back, image_wgrad, text_wgrad)

def reference(image_feats, text_feats, image_head, text_head, image_lse, text_lse):

    def single(index):
        group = (image_feats[index], text_feats[index], image_head, text_head, image_lse[index], text_lse[index])
        return group_grads(group)
    image_back, text_back, image_wgrad, text_wgrad = lax.map(single, jnp.arange(GROUPS, dtype=jnp.int32))
    return (image_back, text_back, lax.optimization_barrier(jnp.sum(image_wgrad, axis=0)), lax.optimization_barrier(jnp.sum(text_wgrad, axis=0)))
```

```python
import functools

import jax
import jax.numpy as jnp
from jax import lax
from jax.experimental import pallas as pl
from jax.experimental.pallas import tpu as pltpu
from jax.sharding import PartitionSpec as P

logit_scale = 50.0
epsilon = 1e-06


def project_head(feats, weight):
    raw = jnp.dot(feats, weight, preferred_element_type=jnp.float32)
    factor = lax.rsqrt(jnp.sum(raw * raw, axis=1, keepdims=True) + epsilon)
    return (raw * factor, factor)


def pre_gradient(embed, factor, grad):
    inner = jnp.sum(embed * grad, axis=1, keepdims=True)
    return (factor * (grad - embed * inner)).astype(jnp.bfloat16)


def weight_tile(left, left_lse, right, right_lse):
    scores = logit_scale * lax.dot_general(
        left, right, (((1,), (1,)), ((), ())), preferred_element_type=jnp.float32
    )
    return (
        0.5 * (jnp.exp(scores - left_lse[:, None]) + jnp.exp(scores - right_lse[None, :]))
    ).astype(jnp.bfloat16)


def shards(image_feats, text_feats, image_head, text_head, image_lse, text_lse):
    image_rows = image_feats[0]
    text_rows = text_feats[0]
    lse_img = image_lse[0]
    lse_txt = text_lse[0]
    image_embed, image_scale = project_head(image_rows, image_head)
    text_embed, text_scale = project_head(text_rows, text_head)
    image_round = image_embed.astype(jnp.bfloat16)
    text_round = text_embed.astype(jnp.bfloat16)
    image_piece = lax.all_gather(image_round, "blk", axis=0, tiled=True)
    image_piece_lse = lax.all_gather(
        lse_img.astype(jnp.bfloat16), "blk", axis=0, tiled=True
    ).astype(jnp.float32)
    text_piece = lax.all_gather(text_round, "blk", axis=0, tiled=True)
    text_piece_lse = lax.all_gather(lse_txt.astype(jnp.bfloat16), "blk", axis=0, tiled=True).astype(
        jnp.float32
    )
    image_weights = weight_tile(image_round, lse_img, text_piece, text_piece_lse)
    image_total_part = jnp.dot(image_weights, text_piece, preferred_element_type=jnp.float32)
    text_weights = weight_tile(image_piece, image_piece_lse, text_round, lse_txt)
    text_total_part = lax.dot_general(
        text_weights, image_piece, (((0,), (0,)), ((), ())), preferred_element_type=jnp.float32
    )
    image_grad = logit_scale * image_total_part - logit_scale * text_round.astype(jnp.float32)
    text_grad = logit_scale * text_total_part - logit_scale * image_round.astype(jnp.float32)
    image_pre = pre_gradient(image_embed, image_scale, image_grad)
    text_pre = pre_gradient(text_embed, text_scale, text_grad)
    image_back = lax.dot_general(
        image_pre, image_head, (((1,), (1,)), ((), ())), preferred_element_type=jnp.float32
    )
    text_back = lax.dot_general(
        text_pre, text_head, (((1,), (1,)), ((), ())), preferred_element_type=jnp.float32
    )
    image_wgrad = lax.dot_general(
        image_rows, image_pre, (((0,), (0,)), ((), ())), preferred_element_type=jnp.float32
    )
    text_wgrad = lax.dot_general(
        text_rows, text_pre, (((0,), (0,)), ((), ())), preferred_element_type=jnp.float32
    )
    image_total, text_total = lax.psum((image_wgrad, text_wgrad), ("blk", "rep"))
    return (image_back[None], text_back[None], image_total, text_total)


MESH = pl.DeviceIdType.MESH
SIDE = 2
NT = (((1,), (1,)), ((), ()))
TN = (((0,), (0,)), ((), ()))


def mm(a, b, dims=(((1,), (0,)), ((), ()))):
    return lax.dot_general(a, b, dims, preferred_element_type=jnp.float32)


def fused(
    nz, chunk,
    xi_in, xt_in, wi_in, wt_in, li, lt,
    back_i, back_t, hi, ht,
    xi, xt, xin, xtn, wi, wt, pre_i, pre_t, got_pre_i, got_pre_t,
    ei, et, ein, etn, fi, ft, fin, ftn,
    im, ip, tm, tp, lip, ltp, u, v, w,
    acc_i, acc_t, acc_in, acc_tn, xit, xtt,
    bufs_low, bufs_high, bufs_t,
    send, recv, local,
):
    n, e = im.shape
    di, dt = wi.shape[0], wt.shape[0]
    count = n // chunk
    b, r = lax.axis_index("blk"), lax.axis_index("rep")
    x, y = lax.rem(b, 2), b // 2
    core, z = lax.rem(r, 2), r // 2
    px = {"blk": y * 2 + 1 - x, "rep": r}
    py = {"blk": (1 - y) * 2 + x, "rep": r}
    pc = {"blk": b, "rep": z * 2 + 1 - core}
    pz = [{"blk": b, "rep": lax.rem(z + k, nz) * 2 + core} for k in range(1, nz)]
    along_x, along_y = y * 2 + 1 - x, (1 - y) * 2 + x
    p_img = {"blk": along_x * (1 - core) + along_y * core, "rep": r}
    p_txt = {"blk": along_y * (1 - core) + along_x * core, "rep": r}

    used = [0]

    def push(src, dst, dev):
        s = used[0]
        used[0] += 1
        copy = pltpu.make_async_remote_copy(
            src_ref=src, dst_ref=dst, send_sem=send.at[s], recv_sem=recv.at[s],
            device_id=dev, device_id_type=MESH,
        )
        copy.start()
        started.append(copy)
        return copy

    started, moved = [], []

    def move(src, dst):
        copy = pltpu.make_async_copy(src, dst, local.at[len(moved)])
        copy.start()
        moved.append(copy)
        return copy

    barrier = pltpu.get_barrier_semaphore()
    for dev in [px, py, pc] + pz:
        pl.semaphore_signal(barrier, inc=1, device_id=dev, device_id_type=MESH)
    loads = [move(wi_in, wi), move(xi_in, xi), move(wt_in, wt), move(xt_in, xt)]
    pl.semaphore_wait(barrier, 2 + nz)
    got_i, got_t = [], []
    got_li = push(li, lip, p_img)
    got_lt = push(lt, ltp, p_txt)
    for c in range(count):
        rows = pl.ds(c * chunk, chunk)
        got_i.append(push(xi_in.at[rows, :], xin.at[rows, :], p_img))
        got_t.append(push(xt_in.at[rows, :], xtn.at[rows, :], p_txt))

    def project(rows, feats, head, embed, factor, rounded):
        raw = mm(feats[rows, :], head[...])
        f = lax.rsqrt(jnp.sum(raw * raw, axis=1, keepdims=True) + epsilon)
        out = raw * f
        embed[rows, :] = out
        factor[rows, :] = f
        rounded[rows, :] = out.astype(jnp.bfloat16)

    for copy in loads[:2]:
        copy.wait()

    @pl.loop(0, count)
    def _(c):
        project(pl.ds(pl.multiple_of(c * chunk, chunk), chunk), xi, wi, ei, fi, im)

    for copy in loads[2:]:
        copy.wait()

    @pl.loop(0, count)
    def _(c):
        project(pl.ds(pl.multiple_of(c * chunk, chunk), chunk), xt, wt, et, ft, tm)

    def columns(lse):
        half = 0.5 * jnp.exp(-lse)
        return jnp.transpose(jnp.broadcast_to(half, (128, n)))

    u[0] = columns(li[...])
    v[0] = 0.5 * jnp.exp(-lt[...])
    images, texts = (im, ip), (tm, tp)

    def tile(p, q, r0, nr, c0, nc):
        s = logit_scale * mm(images[p][pl.ds(r0, nr), :], texts[q][pl.ds(c0, nc), :], NT)
        fac = u[p, pl.ds(r0, nr), :][:, :1] + v[q, :, pl.ds(c0, nc)]
        w[p, q, pl.ds(r0, nr), pl.ds(c0, nc)] = (jnp.exp(s) * fac).astype(jnp.bfloat16)

    @pl.loop(0, count)
    def _(c):
        tile(0, 0, pl.multiple_of(c * chunk, chunk), chunk, 0, n)

    @pl.loop(0, count)
    def _(c):
        rows = pl.ds(pl.multiple_of(c * chunk, chunk), chunk)
        acc_i[rows, :] = mm(w[0, 0, rows, :], tm[...])
        acc_t[rows, :] = mm(w[0, 0, :, rows], im[...], TN)

    for src, dst, width in ((xi, xit, di), (xt, xtt, dt)):

        @pl.loop(0, width // 128)
        def _(k, src=src, dst=dst):
            part = pl.ds(pl.multiple_of(k * 128, 128), 128)
            dst[part, pl.ds(0, n)] = jnp.transpose(src[:, part])

    got_li.wait_recv()
    got_lt.wait_recv()
    u[1] = columns(lip[...])
    v[1] = 0.5 * jnp.exp(-ltp[...])
    for c in range(count):
        rows = pl.ds(c * chunk, chunk)
        later = pl.ds(n + c * chunk, chunk)
        got_i[c].wait_recv()
        project(rows, xin, wi, ein, fin, ip)
        tile(1, 0, c * chunk, chunk, 0, n)
        acc_in[rows, :] = mm(w[1, 0, rows, :], tm[...])
        xit[:, later] = jnp.transpose(xin[rows, :])
        got_t[c].wait_recv()
        project(rows, xtn, wt, etn, ftn, tp)
        tile(0, 1, 0, n, c * chunk, chunk)
        acc_tn[rows, :] = mm(w[0, 1, :, rows], im[...], TN)
        xtt[:, later] = jnp.transpose(xtn[rows, :])
        tile(1, 1, c * chunk, chunk, 0, (c + 1) * chunk)
        if c > 0:
            tile(1, 1, 0, c * chunk, c * chunk, chunk)

    sum_i, sum_t = [], []
    for c in range(count):
        rows = pl.ds(c * chunk, chunk)
        later = pl.ds(n + c * chunk, chunk)
        total = acc_in[rows, :] + mm(w[1, 1, rows, :], tp[...])
        pre_i[later, :] = pre_gradient(ein[rows, :], fin[rows, :], logit_scale * total)
        sum_i.append(push(pre_i.at[later, :], got_pre_i.at[rows, :], p_img))
        total = acc_tn[rows, :] + mm(w[1, 1, :, rows], ip[...], TN)
        pre_t[later, :] = pre_gradient(etn[rows, :], ftn[rows, :], logit_scale * total)
        sum_t.append(push(pre_t.at[later, :], got_pre_t.at[rows, :], p_txt))

    @pl.loop(0, count)
    def _(c):
        rows = pl.ds(pl.multiple_of(c * chunk, chunk), chunk)
        total = acc_i[rows, :] + mm(w[0, 1, rows, :], tp[...])
        grad = logit_scale * total - logit_scale * tm[rows, :].astype(jnp.float32)
        pre_i[rows, :] = pre_gradient(ei[rows, :], fi[rows, :], grad)
        total = acc_t[rows, :] + mm(w[1, 0, :, rows], ip[...], TN)
        grad = logit_scale * total - logit_scale * im[rows, :].astype(jnp.float32)
        pre_t[rows, :] = pre_gradient(et[rows, :], ft[rows, :], grad)

    eh = e // 2

    def added(p, q):
        return (p.astype(jnp.float32) + q.astype(jnp.float32)).astype(jnp.bfloat16)

    ij = ((x, y), (y, x))
    pi, pj = (px, py), (py, px)
    both = range(2)

    def head_half(which, dst, flipped, pre):
        part = dst.shape[4]
        half = flipped.shape[0] // 2
        for q in range(4):
            rows = pl.ds(pl.multiple_of(which * half + q * nz * part, nz * part), nz * part)
            g = mm(flipped[rows, :], pre[...])
            for ab in both:
                for k in range(nz):
                    dst[ab, q // 2, q % 2, k] = g[
                        k * part : (k + 1) * part, ab * eh : (ab + 1) * eh
                    ].astype(jnp.bfloat16)

    def reduce_head(flipped, pre, result, out_half, own, from_core, r1, r2, r3, full):
        head_half(1 - core, out_half, flipped, pre)
        first, second = [
            [push(out_half.at[ab, i], from_core.at[ab, i], pc) for ab, i in places]
            for places in (
                [(ab, 1 - ij[ab][0]) for ab in both],
                [(ab, ij[ab][0]) for ab in both],
            )
        ]
        head_half(core, own, flipped, pre)
        s1 = []
        for ab in both:
            i = ij[ab][0]
            first[ab].wait_recv()
            own[ab, 1 - i] = added(own[ab, 1 - i], from_core[ab, 1 - i])
            s1.append(push(own.at[ab, 1 - i], r1.at[ab], pi[ab]))
        for ab in both:
            i = ij[ab][0]
            second[ab].wait_recv()
            own[ab, i] = added(own[ab, i], from_core[ab, i])
        yield
        s2 = []
        for ab in both:
            i, j = ij[ab]
            s1[ab].wait_recv()
            own[ab, i] = added(own[ab, i], r1[ab])
            s2.append(push(own.at[ab, i, 1 - j], r2.at[ab], pj[ab]))
        yield
        s3 = []
        for ab in both:
            i, j = ij[ab]
            s2[ab].wait_recv()
            own[ab, i, j] = added(own[ab, i, j], r2[ab])
            s3.append(
                [push(own.at[ab, i, j, lax.rem(z + k, nz)], r3.at[ab, k], pz[k - 1]) for k in range(1, nz)]
            )
        yield
        s4 = []
        for ab in both:
            i, j = ij[ab]
            total = own[ab, i, j, z].astype(jnp.float32)
            for k in range(1, nz):
                s3[ab][k - 1].wait_recv()
                total = total + r3[ab, k].astype(jnp.float32)
            full[core, ab, i, j, z] = total.astype(jnp.bfloat16)
            piece = full.at[core, ab, i, j, z]
            s4.append([push(piece, piece, pz[k - 1]) for k in range(1, nz)])
        yield
        s5 = []
        for ab in both:
            i, j = ij[ab]
            for copy in s4[ab]:
                copy.wait_recv()
            piece = full.at[core, ab, i, j]
            s5.append(push(piece, piece, pj[ab]))
        yield
        s6, last = [], []
        for ab in both:
            i, j = ij[ab]
            s5[ab].wait_recv()
            piece = full.at[core, ab, i]
            s6.append(push(piece, piece, pi[ab]))
            last.append(push(piece, piece, pc))
        yield
        for ab in both:
            i, j = ij[ab]
            s6[ab].wait_recv()
            piece = full.at[core, ab, 1 - i]
            last.append(push(piece, piece, pc))
        part = full.shape[5]

        def widen(cc):
            for ab in both:
                for q in range(4):
                    for k in range(nz):
                        first = pl.multiple_of(((cc * 4 + q) * nz + k) * part, part)
                        result[pl.ds(first, part), pl.ds(ab * eh, eh)] = full[
                            cc, ab, q // 2, q % 2, k
                        ].astype(jnp.float32)

        widen(core)
        yield
        for copy in last:
            copy.wait_recv()
        widen(1 - core)
        yield

    low, high = pl.ds(0, di // 2), pl.ds(di // 2, di // 2)
    parts = [
        reduce_head(xtt, pre_t, ht, *bufs_t),
        reduce_head(xit.at[low, :], pre_i, hi.at[low, :], *bufs_low),
        reduce_head(xit.at[high, :], pre_i, hi.at[high, :], *bufs_high),
    ]
    for turn in range(8):
        for step in parts:
            next(step)
        if turn == 3:
            for got, pre, other, head, back in (
                (sum_i, pre_i, got_pre_i, wi, back_i),
                (sum_t, pre_t, got_pre_t, wt, back_t),
            ):
                for copy in got:
                    copy.wait_recv()

                @pl.loop(0, count)
                def _(c, pre=pre, other=other, head=head, back=back):
                    rows = pl.ds(pl.multiple_of(c * chunk, chunk), chunk)
                    back[rows, :] = mm(added(pre[rows, :], other[rows, :]), head[...], NT)

    for copy in started:
        copy.wait_send()


def tail(bi, bt, hi, ht, bi_out, bt_out, hi_out, ht_out, sems):
    copies = [
        pltpu.make_async_copy(src, dst, sems.at[k])
        for k, (src, dst) in enumerate(
            ((bi, bi_out), (bt, bt_out), (hi, hi_out), (ht, ht_out))
        )
    ]
    for copy in copies:
        copy.start()
    for copy in copies:
        copy.wait()


def kernel_shards(nz, image_feats, text_feats, image_head, text_head, image_lse, text_lse):
    n, di = image_feats.shape[1:]
    dt, e = text_head.shape
    chunk = n // 4
    bf, f32 = jnp.bfloat16, jnp.float32
    vm = pltpu.VMEM

    def buffers(rows):
        leads = [(2, 2, 2, nz)] * 3 + [(2, 2, nz), (2, nz), (2, nz), (2, 2, 2, 2, nz)]
        return [vm((*lead, rows // (8 * nz), e // 2), bf) for lead in leads]

    copies = 2 + 4 * (n // chunk) + 3 * (4 + 2 + 2 + 2 * (nz - 1) * 2 + 2 + 2 + 4)
    spec = pl.BlockSpec(memory_space=pltpu.VMEM)
    anywhere = pl.BlockSpec(memory_space=pl.ANY)
    image_back, text_back, image_total, text_total = pl.pallas_call(
        functools.partial(fused, nz, chunk),
        out_shape=[vm((n, di), f32), vm((n, dt), f32), vm((di, e), f32), vm((dt, e), f32)],
        in_specs=[anywhere] * 4 + [spec] * 2,
        out_specs=[spec] * 4,
        scratch_shapes=[
            vm((n, di), bf), vm((n, dt), bf), vm((n, di), bf), vm((n, dt), bf),
            vm((di, e), bf), vm((dt, e), bf),
            vm((2 * n, e), bf), vm((2 * n, e), bf), vm((n, e), bf), vm((n, e), bf),
            vm((n, e), f32), vm((n, e), f32), vm((n, e), f32), vm((n, e), f32),
            vm((n, 1), f32), vm((n, 1), f32), vm((n, 1), f32), vm((n, 1), f32),
            vm((n, e), bf), vm((n, e), bf), vm((n, e), bf), vm((n, e), bf),
            vm((1, n), f32), vm((1, n), f32), vm((2, n, 128), f32), vm((2, 1, n), f32),
            vm((2, 2, n, n), bf),
            vm((n, e), f32), vm((n, e), f32), vm((n, e), f32), vm((n, e), f32),
            vm((di, 2 * n), bf), vm((dt, 2 * n), bf),
            buffers(di // 2), buffers(di // 2), buffers(dt),
            pltpu.SemaphoreType.DMA((copies,)), pltpu.SemaphoreType.DMA((copies,)),
            pltpu.SemaphoreType.DMA((4,)),
        ],
        compiler_params=pltpu.CompilerParams(
            collective_id=0, has_side_effects=True, vmem_limit_bytes=54 * 1024 * 1024
        ),
    )(image_feats[0], text_feats[0], image_head, text_head, image_lse, text_lse)
    shapes = [(n, di), (n, dt), (di, e), (dt, e)]
    image_back, text_back, image_total, text_total = pl.pallas_call(
        tail,
        out_shape=[jax.ShapeDtypeStruct(shape, f32) for shape in shapes],
        in_specs=[spec] * 4,
        out_specs=[anywhere] * 4,
        scratch_shapes=[pltpu.SemaphoreType.DMA((4,))],
        compiler_params=pltpu.CompilerParams(vmem_limit_bytes=4 * 1024 * 1024),
    )(image_back, text_back, image_total, text_total)
    return (image_back[None], text_back[None], image_total, text_total)


def solution(mesh):
    blk, rep = mesh.shape["blk"], mesh.shape["rep"]
    body = shards
    if blk == SIDE * SIDE and rep % SIDE == 0:
        body = functools.partial(kernel_shards, rep // SIDE)
    return jax.shard_map(
        body,
        mesh=mesh,
        in_specs=(
            P("rep", "blk", None),
            P("rep", "blk", None),
            P(),
            P(),
            P("rep", "blk"),
            P("rep", "blk"),
        ),
        out_specs=(P("rep", "blk", None), P("rep", "blk", None), P(), P()),
        check_vma=False,
    )
```

```python
import functools

import jax
import jax.numpy as jnp
from jax import lax
from jax.experimental import pallas as pl
from jax.experimental.pallas import tpu as pltpu
from jax.sharding import PartitionSpec as P

logit_scale = 50.0
epsilon = 1e-06


def project_head(feats, weight):
    raw = jnp.dot(feats, weight, preferred_element_type=jnp.float32)
    factor = lax.rsqrt(jnp.sum(raw * raw, axis=1, keepdims=True) + epsilon)
    return (raw * factor, factor)


def pre_gradient(embed, factor, grad):
    inner = jnp.sum(embed * grad, axis=1, keepdims=True)
    return (factor * (grad - embed * inner)).astype(jnp.bfloat16)


def weight_tile(left, left_lse, right, right_lse):
    scores = logit_scale * lax.dot_general(
        left, right, (((1,), (1,)), ((), ())), preferred_element_type=jnp.float32
    )
    return (
        0.5 * (jnp.exp(scores - left_lse[:, None]) + jnp.exp(scores - right_lse[None, :]))
    ).astype(jnp.bfloat16)


def shards(image_feats, text_feats, image_head, text_head, image_lse, text_lse):
    image_rows = image_feats[0]
    text_rows = text_feats[0]
    lse_img = image_lse[0]
    lse_txt = text_lse[0]
    image_embed, image_scale = project_head(image_rows, image_head)
    text_embed, text_scale = project_head(text_rows, text_head)
    image_round = image_embed.astype(jnp.bfloat16)
    text_round = text_embed.astype(jnp.bfloat16)
    image_piece = lax.all_gather(image_round, "blk", axis=0, tiled=True)
    image_piece_lse = lax.all_gather(
        lse_img.astype(jnp.bfloat16), "blk", axis=0, tiled=True
    ).astype(jnp.float32)
    text_piece = lax.all_gather(text_round, "blk", axis=0, tiled=True)
    text_piece_lse = lax.all_gather(lse_txt.astype(jnp.bfloat16), "blk", axis=0, tiled=True).astype(
        jnp.float32
    )
    image_weights = weight_tile(image_round, lse_img, text_piece, text_piece_lse)
    image_total_part = jnp.dot(image_weights, text_piece, preferred_element_type=jnp.float32)
    text_weights = weight_tile(image_piece, image_piece_lse, text_round, lse_txt)
    text_total_part = lax.dot_general(
        text_weights, image_piece, (((0,), (0,)), ((), ())), preferred_element_type=jnp.float32
    )
    image_grad = logit_scale * image_total_part - logit_scale * text_round.astype(jnp.float32)
    text_grad = logit_scale * text_total_part - logit_scale * image_round.astype(jnp.float32)
    image_pre = pre_gradient(image_embed, image_scale, image_grad)
    text_pre = pre_gradient(text_embed, text_scale, text_grad)
    image_back = lax.dot_general(
        image_pre, image_head, (((1,), (1,)), ((), ())), preferred_element_type=jnp.float32
    )
    text_back = lax.dot_general(
        text_pre, text_head, (((1,), (1,)), ((), ())), preferred_element_type=jnp.float32
    )
    image_wgrad = lax.dot_general(
        image_rows, image_pre, (((0,), (0,)), ((), ())), preferred_element_type=jnp.float32
    )
    text_wgrad = lax.dot_general(
        text_rows, text_pre, (((0,), (0,)), ((), ())), preferred_element_type=jnp.float32
    )
    image_total, text_total = lax.psum((image_wgrad, text_wgrad), ("blk", "rep"))
    return (image_back[None], text_back[None], image_total, text_total)


MESH = pl.DeviceIdType.MESH
SIDE = 2
WIDE_I, WIDE_T = 256, 768
IMAGE = 3.1
BACK_T = 21.0
BACK_I = 21.1
EARLY_T = 1
EARLY_I = 0
SEND_T = 10.8
SEND_I = 10.9
GAP = 0.01
STEP = 0.8
STAGES = (0.0, 2.5, 6.0, 9.0, 12.5, 16.0, 19.0, 22.5, 25.0)
NT = (((1,), (1,)), ((), ()))
TN = (((0,), (0,)), ((), ()))


def mm(a, b, dims=(((1,), (0,)), ((), ()))):
    return lax.dot_general(a, b, dims, preferred_element_type=jnp.float32)


def fused(
    nz, chunk,
    xi_in, xt_in, wi_in, wt_in, li, lt,
    back_i, back_t, hi, ht,
    xi, xt, xin, xtn, wi, wt, pre_i, pre_t, got_pre_i, got_pre_t,
    ei, et, ein, etn, fi, ft, fin, ftn,
    im, ip, tm, tp, lip, ltp, u, v, w,
    acc_i, acc_t, acc_in, acc_tn, xit, xtt,
    bufs_i, bufs_t,
    send, recv, local,
):
    n, e = im.shape
    di, dt = wi.shape[0], wt.shape[0]
    count = n // chunk
    b, r = lax.axis_index("blk"), lax.axis_index("rep")
    x, y = lax.rem(b, 2), b // 2
    core, z = lax.rem(r, 2), r // 2
    px = {"blk": y * 2 + 1 - x, "rep": r}
    py = {"blk": (1 - y) * 2 + x, "rep": r}
    pc = {"blk": b, "rep": z * 2 + 1 - core}
    pz = [{"blk": b, "rep": lax.rem(z + k, nz) * 2 + core} for k in range(1, nz)]
    along_x, along_y = y * 2 + 1 - x, (1 - y) * 2 + x
    p_img = {"blk": along_x * (1 - core) + along_y * core, "rep": r}
    p_txt = {"blk": along_y * (1 - core) + along_x * core, "rep": r}

    used = [0]

    def push(src, dst, dev):
        s = used[0]
        used[0] += 1
        copy = pltpu.make_async_remote_copy(
            src_ref=src, dst_ref=dst, send_sem=send.at[s], recv_sem=recv.at[s],
            device_id=dev, device_id_type=MESH,
        )
        copy.start()
        started.append(copy)
        return copy

    started, moved = [], []

    def move(src, dst):
        copy = pltpu.make_async_copy(src, dst, local.at[len(moved)])
        copy.start()
        moved.append(copy)
        return copy

    barrier = pltpu.get_barrier_semaphore()
    for dev in [px, py, pc] + pz:
        pl.semaphore_signal(barrier, inc=1, device_id=dev, device_id_type=MESH)
    loads = [move(wi_in, wi), move(xi_in, xi), move(wt_in, wt), move(xt_in, xt)]
    pl.semaphore_wait(barrier, 2 + nz)
    got_i, got_t = [], []
    got_li = push(li, lip, p_img)
    got_lt = push(lt, ltp, p_txt)
    for c in range(count):
        rows = pl.ds(c * chunk, chunk)
        got_i.append(push(xi_in.at[rows, :], xin.at[rows, :], p_img))
        got_t.append(push(xt_in.at[rows, :], xtn.at[rows, :], p_txt))

    def project(rows, feats, head, embed, factor, rounded):
        raw = mm(feats[rows, :], head[...])
        f = lax.rsqrt(jnp.sum(raw * raw, axis=1, keepdims=True) + epsilon)
        out = raw * f
        embed[rows, :] = out
        factor[rows, :] = f
        rounded[rows, :] = out.astype(jnp.bfloat16)

    for copy in loads[:2]:
        copy.wait()

    @pl.loop(0, count)
    def _(c):
        project(pl.ds(pl.multiple_of(c * chunk, chunk), chunk), xi, wi, ei, fi, im)

    for copy in loads[2:]:
        copy.wait()

    @pl.loop(0, count)
    def _(c):
        project(pl.ds(pl.multiple_of(c * chunk, chunk), chunk), xt, wt, et, ft, tm)

    def columns(lse):
        half = 0.5 * jnp.exp(-lse)
        return jnp.transpose(jnp.broadcast_to(half, (128, n)))

    u[0] = columns(li[...])
    v[0] = 0.5 * jnp.exp(-lt[...])
    images, texts = (im, ip), (tm, tp)

    def tile(p, q, r0, nr, c0, nc):
        s = logit_scale * mm(images[p][pl.ds(r0, nr), :], texts[q][pl.ds(c0, nc), :], NT)
        fac = u[p, pl.ds(r0, nr), :][:, :1] + v[q, :, pl.ds(c0, nc)]
        w[p, q, pl.ds(r0, nr), pl.ds(c0, nc)] = (jnp.exp(s) * fac).astype(jnp.bfloat16)

    @pl.loop(0, count)
    def _(c):
        tile(0, 0, pl.multiple_of(c * chunk, chunk), chunk, 0, n)

    @pl.loop(0, count)
    def _(c):
        rows = pl.ds(pl.multiple_of(c * chunk, chunk), chunk)
        acc_i[rows, :] = mm(w[0, 0, rows, :], tm[...])
        acc_t[rows, :] = mm(w[0, 0, :, rows], im[...], TN)

    for src, dst, width in ((xi, xit, di), (xt, xtt, dt)):

        @pl.loop(0, width // 128)
        def _(k, src=src, dst=dst):
            part = pl.ds(pl.multiple_of(k * 128, 128), 128)
            dst[part, pl.ds(0, n)] = jnp.transpose(src[:, part])

    got_li.wait_recv()
    got_lt.wait_recv()
    u[1] = columns(lip[...])
    v[1] = 0.5 * jnp.exp(-ltp[...])
    for c in range(count):
        rows = pl.ds(c * chunk, chunk)
        later = pl.ds(n + c * chunk, chunk)
        got_i[c].wait_recv()
        project(rows, xin, wi, ein, fin, ip)
        tile(1, 0, c * chunk, chunk, 0, n)
        acc_in[rows, :] = mm(w[1, 0, rows, :], tm[...])
        xit[:, later] = jnp.transpose(xin[rows, :])
        got_t[c].wait_recv()
        project(rows, xtn, wt, etn, ftn, tp)
        tile(0, 1, 0, n, c * chunk, chunk)
        acc_tn[rows, :] = mm(w[0, 1, :, rows], im[...], TN)
        xtt[:, later] = jnp.transpose(xtn[rows, :])
        tile(1, 1, c * chunk, chunk, 0, (c + 1) * chunk)
        if c > 0:
            tile(1, 1, 0, c * chunk, c * chunk, chunk)

    sum_i, sum_t = [], []

    def texts_of_neighbour():
        block = 2 * chunk
        for c in range(n // block):
            rows, later = pl.ds(c * block, block), pl.ds(n + c * block, block)
            total = acc_tn[rows, :] + mm(w[1, 1, :, rows], ip[...], TN)
            pre_t[later, :] = pre_gradient(etn[rows, :], ftn[rows, :], logit_scale * total)
            for k in range(2 * c, min(2 * c + 2, EARLY_T)):
                send_texts(k)

    def images_of_neighbour():
        block = 2 * chunk
        for c in range(n // block):
            rows, later = pl.ds(c * block, block), pl.ds(n + c * block, block)
            total = acc_in[rows, :] + mm(w[1, 1, rows, :], tp[...])
            pre_i[later, :] = pre_gradient(ein[rows, :], fin[rows, :], logit_scale * total)
            for k in range(2 * c, min(2 * c + 2, EARLY_I)):
                send_images(k)

    def send_images(c):
        rows, later = pl.ds(c * chunk, chunk), pl.ds(n + c * chunk, chunk)
        sum_i.append(push(pre_i.at[later, :], got_pre_i.at[rows, :], p_img))

    def send_texts(c):
        rows, later = pl.ds(c * chunk, chunk), pl.ds(n + c * chunk, chunk)
        sum_t.append(push(pre_t.at[later, :], got_pre_t.at[rows, :], p_txt))

    def own_texts():
        for c in range(2):
            rows = pl.ds(c * (n // 2), n // 2)
            total = acc_t[rows, :] + mm(w[1, 0, :, rows], ip[...], TN)
            grad = logit_scale * total - logit_scale * im[rows, :].astype(jnp.float32)
            pre_t[rows, :] = pre_gradient(et[rows, :], ft[rows, :], grad)

    def own_images():
        for c in range(2):
            rows = pl.ds(c * (n // 2), n // 2)
            total = acc_i[rows, :] + mm(w[0, 1, rows, :], tp[...])
            grad = logit_scale * total - logit_scale * tm[rows, :].astype(jnp.float32)
            pre_i[rows, :] = pre_gradient(ei[rows, :], fi[rows, :], grad)


    def added(p, q):
        return (p.astype(jnp.float32) + q.astype(jnp.float32)).astype(jnp.bfloat16)

    ij = ((x, y), (y, x))
    pi, pj = (px, py), (py, px)
    both = range(2)

    def head_half(which, dst, flipped, pre, first):
        part, eh = dst.shape[4:]
        half = flipped.shape[0] // 2
        rows = pl.ds(pl.multiple_of(which * half, half), half)
        g = mm(flipped[rows, :], pre[:, pl.ds(first, 2 * eh)])
        for q in range(4):
            for ab in both:
                for k in range(nz):
                    row = (q * nz + k) * part
                    dst[ab, q // 2, q % 2, k] = g[
                        row : row + part, ab * eh : (ab + 1) * eh
                    ].astype(jnp.bfloat16)

    def reduce_head(flipped, pre, result, first_column, bufs):
        out_half, own, from_core, r1, r2, r3, full = bufs
        head_half(1 - core, out_half, flipped, pre, first_column)
        first, second = [
            [push(out_half.at[ab, i], from_core.at[ab, i], pc) for ab, i in places]
            for places in (
                [(ab, 1 - ij[ab][0]) for ab in both],
                [(ab, ij[ab][0]) for ab in both],
            )
        ]
        head_half(core, own, flipped, pre, first_column)
        yield
        s1 = []
        for ab in both:
            i = ij[ab][0]
            first[ab].wait_recv()
            own[ab, 1 - i] = added(own[ab, 1 - i], from_core[ab, 1 - i])
            s1.append(push(own.at[ab, 1 - i], r1.at[ab], pi[ab]))
        for ab in both:
            i = ij[ab][0]
            second[ab].wait_recv()
            own[ab, i] = added(own[ab, i], from_core[ab, i])
        yield
        s2 = []
        for ab in both:
            i, j = ij[ab]
            s1[ab].wait_recv()
            own[ab, i] = added(own[ab, i], r1[ab])
            s2.append(push(own.at[ab, i, 1 - j], r2.at[ab], pj[ab]))
        yield
        s3 = []
        for ab in both:
            i, j = ij[ab]
            s2[ab].wait_recv()
            own[ab, i, j] = added(own[ab, i, j], r2[ab])
            s3.append(
                [push(own.at[ab, i, j, lax.rem(z + k, nz)], r3.at[ab, k], pz[k - 1]) for k in range(1, nz)]
            )
        yield
        s4 = []
        for ab in both:
            i, j = ij[ab]
            total = own[ab, i, j, z].astype(jnp.float32)
            for k in range(1, nz):
                s3[ab][k - 1].wait_recv()
                total = total + r3[ab, k].astype(jnp.float32)
            full[core, ab, i, j, z] = total.astype(jnp.bfloat16)
            piece = full.at[core, ab, i, j, z]
            s4.append([push(piece, piece, pz[k - 1]) for k in range(1, nz)])
        yield
        s5 = []
        for ab in both:
            i, j = ij[ab]
            for copy in s4[ab]:
                copy.wait_recv()
            piece = full.at[core, ab, i, j]
            s5.append(push(piece, piece, pj[ab]))
        yield
        s6, last = [], []
        for ab in both:
            i, j = ij[ab]
            s5[ab].wait_recv()
            piece = full.at[core, ab, i]
            s6.append(push(piece, piece, pi[ab]))
            last.append(push(piece, piece, pc))
        yield
        for ab in both:
            i, j = ij[ab]
            s6[ab].wait_recv()
            piece = full.at[core, ab, 1 - i]
            last.append(push(piece, piece, pc))
        part, eh = full.shape[5:]

        def widen(cc):
            for ab in both:
                for q in range(4):
                    for k in range(nz):
                        first = pl.multiple_of(((cc * 4 + q) * nz + k) * part, part)
                        result[pl.ds(first, part), pl.ds(first_column + ab * eh, eh)] = full[
                            cc, ab, q // 2, q % 2, k
                        ].astype(jnp.float32)

        widen(core)
        yield
        for copy in last:
            copy.wait_recv()
        widen(1 - core)
        yield

    def back(got, pre, other, head, out):
        for copy in got:
            copy.wait_recv()

        @pl.loop(0, count)
        def _(c):
            rows = pl.ds(pl.multiple_of(c * chunk, chunk), chunk)
            out[rows, :] = mm(added(pre[rows, :], other[rows, :]), head[...], NT)

    actions = [
        (-3.0, texts_of_neighbour),
        (-2.0, own_texts),
        (IMAGE - 2.0, images_of_neighbour),
        (IMAGE - 1.0, own_images),
        (BACK_T, functools.partial(back, sum_t, pre_t, got_pre_t, wt, back_t)),
        (BACK_I, functools.partial(back, sum_i, pre_i, got_pre_i, wi, back_i)),
    ]
    for c in range(EARLY_T, count):
        actions.append((SEND_T + c * GAP, functools.partial(send_texts, c)))
    for c in range(EARLY_I, count):
        actions.append((SEND_I + c * GAP, functools.partial(send_images, c)))
    for flipped, pre, result, bufs, start in (
        (xtt, pre_t, ht, bufs_t, 0.0),
        (xit, pre_i, hi, bufs_i, IMAGE),
    ):
        for k in range(bufs[0].shape[0]):
            wide = 2 * bufs[0].shape[-1]
            steps = reduce_head(flipped, pre, result, k * wide, [ref.at[k] for ref in bufs])
            for stage, at in enumerate(STAGES):
                actions.append((start + STEP * k + at, functools.partial(next, steps)))
    for _, action in sorted(actions, key=lambda item: item[0]):
        action()
    for copy in started:
        copy.wait_send()


def tail(bi, bt, hi, ht, bi_out, bt_out, hi_out, ht_out, sems):
    copies = [
        pltpu.make_async_copy(src, dst, sems.at[k])
        for k, (src, dst) in enumerate(
            ((bi, bi_out), (bt, bt_out), (hi, hi_out), (ht, ht_out))
        )
    ]
    for copy in copies:
        copy.start()
    for copy in copies:
        copy.wait()


def kernel_shards(nz, image_feats, text_feats, image_head, text_head, image_lse, text_lse):
    n, di = image_feats.shape[1:]
    dt, e = text_head.shape
    chunk = n // 4
    bf, f32 = jnp.bfloat16, jnp.float32
    vm = pltpu.VMEM

    def buffers(rows, wide):
        leads = [(2, 2, 2, nz)] * 3 + [(2, 2, nz), (2, nz), (2, nz), (2, 2, 2, 2, nz)]
        return [vm((e // wide, *lead, rows // (8 * nz), wide // 2), bf) for lead in leads]

    copies = 2 + 4 * (n // chunk) + (e // WIDE_I + e // WIDE_T) * (4 + 2 + 2 + 2 * (nz - 1) * 2 + 2 + 2 + 4)
    spec = pl.BlockSpec(memory_space=pltpu.VMEM)
    anywhere = pl.BlockSpec(memory_space=pl.ANY)
    image_back, text_back, image_total, text_total = pl.pallas_call(
        functools.partial(fused, nz, chunk),
        out_shape=[vm((n, di), f32), vm((n, dt), f32), vm((di, e), f32), vm((dt, e), f32)],
        in_specs=[anywhere] * 4 + [spec] * 2,
        out_specs=[spec] * 4,
        scratch_shapes=[
            vm((n, di), bf), vm((n, dt), bf), vm((n, di), bf), vm((n, dt), bf),
            vm((di, e), bf), vm((dt, e), bf),
            vm((2 * n, e), bf), vm((2 * n, e), bf), vm((n, e), bf), vm((n, e), bf),
            vm((n, e), f32), vm((n, e), f32), vm((n, e), f32), vm((n, e), f32),
            vm((n, 1), f32), vm((n, 1), f32), vm((n, 1), f32), vm((n, 1), f32),
            vm((n, e), bf), vm((n, e), bf), vm((n, e), bf), vm((n, e), bf),
            vm((1, n), f32), vm((1, n), f32), vm((2, n, 128), f32), vm((2, 1, n), f32),
            vm((2, 2, n, n), bf),
            vm((n, e), f32), vm((n, e), f32), vm((n, e), f32), vm((n, e), f32),
            vm((di, 2 * n), bf), vm((dt, 2 * n), bf),
            buffers(di, WIDE_I), buffers(dt, WIDE_T),
            pltpu.SemaphoreType.DMA((copies,)), pltpu.SemaphoreType.DMA((copies,)),
            pltpu.SemaphoreType.DMA((4,)),
        ],
        compiler_params=pltpu.CompilerParams(
            collective_id=0, has_side_effects=True, vmem_limit_bytes=54 * 1024 * 1024
        ),
    )(image_feats[0], text_feats[0], image_head, text_head, image_lse, text_lse)
    shapes = [(n, di), (n, dt), (di, e), (dt, e)]
    image_back, text_back, image_total, text_total = pl.pallas_call(
        tail,
        out_shape=[jax.ShapeDtypeStruct(shape, f32) for shape in shapes],
        in_specs=[spec] * 4,
        out_specs=[anywhere] * 4,
        scratch_shapes=[pltpu.SemaphoreType.DMA((4,))],
        compiler_params=pltpu.CompilerParams(vmem_limit_bytes=4 * 1024 * 1024),
    )(image_back, text_back, image_total, text_total)
    return (image_back[None], text_back[None], image_total, text_total)


def solution(mesh):
    blk, rep = mesh.shape["blk"], mesh.shape["rep"]
    body = shards
    if blk == SIDE * SIDE and rep % SIDE == 0:
        body = functools.partial(kernel_shards, rep // SIDE)
    return jax.shard_map(
        body,
        mesh=mesh,
        in_specs=(
            P("rep", "blk", None),
            P("rep", "blk", None),
            P(),
            P(),
            P("rep", "blk"),
            P("rep", "blk"),
        ),
        out_specs=(P("rep", "blk", None), P("rep", "blk", None), P(), P()),
        check_vma=False,
    )
```

```python
import functools

import jax
import jax.numpy as jnp
from jax import lax
from jax.experimental import pallas as pl
from jax.experimental.pallas import tpu as pltpu
from jax.sharding import PartitionSpec as P

logit_scale = 50.0
epsilon = 1e-06


def project_head(feats, weight):
    raw = jnp.dot(feats, weight, preferred_element_type=jnp.float32)
    factor = lax.rsqrt(jnp.sum(raw * raw, axis=1, keepdims=True) + epsilon)
    return (raw * factor, factor)


def pre_gradient(embed, factor, grad):
    inner = jnp.sum(embed * grad, axis=1, keepdims=True)
    return (factor * (grad - embed * inner)).astype(jnp.bfloat16)


def weight_tile(left, left_lse, right, right_lse):
    scores = logit_scale * lax.dot_general(
        left, right, (((1,), (1,)), ((), ())), preferred_element_type=jnp.float32
    )
    return (
        0.5 * (jnp.exp(scores - left_lse[:, None]) + jnp.exp(scores - right_lse[None, :]))
    ).astype(jnp.bfloat16)


def shards(image_feats, text_feats, image_head, text_head, image_lse, text_lse):
    image_rows = image_feats[0]
    text_rows = text_feats[0]
    lse_img = image_lse[0]
    lse_txt = text_lse[0]
    image_embed, image_scale = project_head(image_rows, image_head)
    text_embed, text_scale = project_head(text_rows, text_head)
    image_round = image_embed.astype(jnp.bfloat16)
    text_round = text_embed.astype(jnp.bfloat16)
    image_piece = lax.all_gather(image_round, "blk", axis=0, tiled=True)
    image_piece_lse = lax.all_gather(
        lse_img.astype(jnp.bfloat16), "blk", axis=0, tiled=True
    ).astype(jnp.float32)
    text_piece = lax.all_gather(text_round, "blk", axis=0, tiled=True)
    text_piece_lse = lax.all_gather(lse_txt.astype(jnp.bfloat16), "blk", axis=0, tiled=True).astype(
        jnp.float32
    )
    image_weights = weight_tile(image_round, lse_img, text_piece, text_piece_lse)
    image_total_part = jnp.dot(image_weights, text_piece, preferred_element_type=jnp.float32)
    text_weights = weight_tile(image_piece, image_piece_lse, text_round, lse_txt)
    text_total_part = lax.dot_general(
        text_weights, image_piece, (((0,), (0,)), ((), ())), preferred_element_type=jnp.float32
    )
    image_grad = logit_scale * image_total_part - logit_scale * text_round.astype(jnp.float32)
    text_grad = logit_scale * text_total_part - logit_scale * image_round.astype(jnp.float32)
    image_pre = pre_gradient(image_embed, image_scale, image_grad)
    text_pre = pre_gradient(text_embed, text_scale, text_grad)
    image_back = lax.dot_general(
        image_pre, image_head, (((1,), (1,)), ((), ())), preferred_element_type=jnp.float32
    )
    text_back = lax.dot_general(
        text_pre, text_head, (((1,), (1,)), ((), ())), preferred_element_type=jnp.float32
    )
    image_wgrad = lax.dot_general(
        image_rows, image_pre, (((0,), (0,)), ((), ())), preferred_element_type=jnp.float32
    )
    text_wgrad = lax.dot_general(
        text_rows, text_pre, (((0,), (0,)), ((), ())), preferred_element_type=jnp.float32
    )
    image_total, text_total = lax.psum((image_wgrad, text_wgrad), ("blk", "rep"))
    return (image_back[None], text_back[None], image_total, text_total)


MESH = pl.DeviceIdType.MESH
SIDE = 2
KINDS_I, KINDS_T = "znn", "nnn"
ORDER = (
    ("near", "t", 0),
    ("send", "t", 1),
    ("near", "t", 1),
    ("send", "t", 2),
    ("near", "i", 0),
    ("own", "i", 0),
    ("own", "t", 0),
    ("near", "i", 1),
    ("send", "i", 2),
    ("step", "t", 1),
    ("step", "i", 1),
    ("step", "t", 1),
    ("step", "i", 0),
    ("step", "i", 1),
    ("step", "t", 0),
    ("step", "i", 0),
    ("step", "i", 2),
    ("step", "t", 0),
    ("step", "i", 2),
    ("step", "t", 1),
    ("step", "t", 2),
    ("back", "i", 2),
    ("step", "t", 0),
    ("step", "t", 2),
    ("step", "i", 1),
    ("step", "t", 1),
    ("step", "i", 0),
    ("send", "i", 1),
    ("step", "t", 0),
    ("step", "i", 1),
    ("send", "i", 0),
    ("step", "t", 1),
    ("step", "t", 2),
    ("step", "i", 0),
    ("step", "i", 2),
    ("send", "i", 3),
    ("step", "t", 0),
    ("step", "i", 1),
    ("back", "i", 1),
    ("step", "t", 2),
    ("step", "t", 1),
    ("back", "t", 2),
    ("step", "i", 0),
    ("step", "t", 0),
    ("send", "t", 3),
    ("step", "i", 2),
    ("step", "t", 2),
    ("step", "i", 2),
    ("step", "i", 0),
    ("step", "t", 1),
    ("step", "i", 1),
    ("step", "t", 0),
    ("step", "t", 2),
    ("step", "i", 2),
    ("step", "i", 0),
    ("back", "i", 0),
    ("step", "i", 1),
    ("step", "t", 2),
    ("step", "i", 2),
    ("step", "i", 1),
    ("step", "t", 0),
    ("step", "t", 1),
    ("back", "i", 3),
    ("send", "t", 0),
    ("step", "i", 0),
    ("step", "t", 2),
    ("step", "i", 2),
    ("step", "i", 0),
    ("back", "t", 1),
    ("back", "t", 3),
    ("step", "t", 2),
    ("step", "t", 1),
    ("step", "i", 1),
    ("step", "i", 2),
    ("step", "t", 0),
    ("back", "t", 0),
)
NT = (((1,), (1,)), ((), ()))
TN = (((0,), (0,)), ((), ()))


def mm(a, b, dims=(((1,), (0,)), ((), ()))):
    return lax.dot_general(a, b, dims, preferred_element_type=jnp.float32)


def fused(
    nz, chunk,
    xi_in, xt_in, wi_in, wt_in, li, lt,
    back_i, back_t, hi, ht,
    xi, xt, xin, xtn, wi, wt, pre_i, pre_t, got_pre_i, got_pre_t,
    ei, et, ein, etn, fi, ft, fin, ftn,
    im, ip, tm, tp, lip, ltp, u, v, w,
    acc_i, acc_t, acc_in, acc_tn, xit, xtt,
    bufs_i, bufs_t,
    send, recv, local,
):
    n, e = im.shape
    di, dt = wi.shape[0], wt.shape[0]
    count = n // chunk
    b, r = lax.axis_index("blk"), lax.axis_index("rep")
    x, y = lax.rem(b, 2), b // 2
    core, z = lax.rem(r, 2), r // 2
    px = {"blk": y * 2 + 1 - x, "rep": r}
    py = {"blk": (1 - y) * 2 + x, "rep": r}
    pc = {"blk": b, "rep": z * 2 + 1 - core}
    pz = [{"blk": b, "rep": lax.rem(z + k, nz) * 2 + core} for k in range(1, nz)]
    along_x, along_y = y * 2 + 1 - x, (1 - y) * 2 + x
    p_img = {"blk": along_x * (1 - core) + along_y * core, "rep": r}
    p_txt = {"blk": along_y * (1 - core) + along_x * core, "rep": r}

    used = [0]

    def push(src, dst, dev):
        s = used[0]
        used[0] += 1
        copy = pltpu.make_async_remote_copy(
            src_ref=src, dst_ref=dst, send_sem=send.at[s], recv_sem=recv.at[s],
            device_id=dev, device_id_type=MESH,
        )
        copy.start()
        started.append(copy)
        return copy

    started, moved = [], []

    def move(src, dst):
        copy = pltpu.make_async_copy(src, dst, local.at[len(moved)])
        copy.start()
        moved.append(copy)
        return copy

    barrier = pltpu.get_barrier_semaphore()
    for dev in [px, py, pc] + pz:
        pl.semaphore_signal(barrier, inc=1, device_id=dev, device_id_type=MESH)
    loads = [move(wi_in, wi), move(xi_in, xi), move(wt_in, wt), move(xt_in, xt)]
    pl.semaphore_wait(barrier, 2 + nz)
    got_i, got_t = [], []
    got_li = push(li, lip, p_img)
    got_lt = push(lt, ltp, p_txt)
    for c in range(count):
        rows = pl.ds(c * chunk, chunk)
        got_i.append(push(xi_in.at[rows, :], xin.at[rows, :], p_img))
        got_t.append(push(xt_in.at[rows, :], xtn.at[rows, :], p_txt))

    def project(rows, feats, head, embed, factor, rounded):
        raw = mm(feats[rows, :], head[...])
        f = lax.rsqrt(jnp.sum(raw * raw, axis=1, keepdims=True) + epsilon)
        out = raw * f
        embed[rows, :] = out
        factor[rows, :] = f
        rounded[rows, :] = out.astype(jnp.bfloat16)

    for copy in loads[:2]:
        copy.wait()

    @pl.loop(0, count)
    def _(c):
        project(pl.ds(pl.multiple_of(c * chunk, chunk), chunk), xi, wi, ei, fi, im)

    for copy in loads[2:]:
        copy.wait()

    @pl.loop(0, count)
    def _(c):
        project(pl.ds(pl.multiple_of(c * chunk, chunk), chunk), xt, wt, et, ft, tm)

    def columns(lse):
        half = 0.5 * jnp.exp(-lse)
        return jnp.transpose(jnp.broadcast_to(half, (128, n)))

    u[0] = columns(li[...])
    v[0] = 0.5 * jnp.exp(-lt[...])
    images, texts = (im, ip), (tm, tp)

    def tile(p, q, r0, nr, c0, nc):
        s = logit_scale * mm(images[p][pl.ds(r0, nr), :], texts[q][pl.ds(c0, nc), :], NT)
        fac = u[p, pl.ds(r0, nr), :][:, :1] + v[q, :, pl.ds(c0, nc)]
        w[p, q, pl.ds(r0, nr), pl.ds(c0, nc)] = (jnp.exp(s) * fac).astype(jnp.bfloat16)

    @pl.loop(0, count)
    def _(c):
        tile(0, 0, pl.multiple_of(c * chunk, chunk), chunk, 0, n)

    @pl.loop(0, count)
    def _(c):
        rows = pl.ds(pl.multiple_of(c * chunk, chunk), chunk)
        acc_i[rows, :] = mm(w[0, 0, rows, :], tm[...])
        acc_t[rows, :] = mm(w[0, 0, :, rows], im[...], TN)

    for src, dst, width in ((xi, xit, di), (xt, xtt, dt)):

        @pl.loop(0, width // 128)
        def _(k, src=src, dst=dst):
            part = pl.ds(pl.multiple_of(k * 128, 128), 128)
            dst[part, pl.ds(0, n)] = jnp.transpose(src[:, part])

    got_li.wait_recv()
    got_lt.wait_recv()
    u[1] = columns(lip[...])
    v[1] = 0.5 * jnp.exp(-ltp[...])
    for c in range(count):
        rows = pl.ds(c * chunk, chunk)
        later = pl.ds(n + c * chunk, chunk)
        got_i[c].wait_recv()
        project(rows, xin, wi, ein, fin, ip)
        tile(1, 0, c * chunk, chunk, 0, n)
        acc_in[rows, :] = mm(w[1, 0, rows, :], tm[...])
        xit[:, later] = jnp.transpose(xin[rows, :])
        got_t[c].wait_recv()
        project(rows, xtn, wt, etn, ftn, tp)
        tile(0, 1, 0, n, c * chunk, chunk)
        acc_tn[rows, :] = mm(w[0, 1, :, rows], im[...], TN)
        xtt[:, later] = jnp.transpose(xtn[rows, :])
        tile(1, 1, c * chunk, chunk, 0, (c + 1) * chunk)
        if c > 0:
            tile(1, 1, 0, c * chunk, c * chunk, chunk)

    sums = {}
    block = n // 2

    def texts_of_neighbour(c):
        rows, later = pl.ds(c * block, block), pl.ds(n + c * block, block)
        total = acc_tn[rows, :] + mm(w[1, 1, :, rows], ip[...], TN)
        pre_t[later, :] = pre_gradient(etn[rows, :], ftn[rows, :], logit_scale * total)

    def images_of_neighbour(c):
        rows, later = pl.ds(c * block, block), pl.ds(n + c * block, block)
        total = acc_in[rows, :] + mm(w[1, 1, rows, :], tp[...])
        pre_i[later, :] = pre_gradient(ein[rows, :], fin[rows, :], logit_scale * total)

    def send_sum(head, c):
        rows, later = pl.ds(c * chunk, chunk), pl.ds(n + c * chunk, chunk)
        if head == "t":
            sums[head, c] = push(pre_t.at[later, :], got_pre_t.at[rows, :], p_txt)
        else:
            sums[head, c] = push(pre_i.at[later, :], got_pre_i.at[rows, :], p_img)

    def own_texts():
        for c in range(2):
            rows = pl.ds(c * (n // 2), n // 2)
            total = acc_t[rows, :] + mm(w[1, 0, :, rows], ip[...], TN)
            grad = logit_scale * total - logit_scale * im[rows, :].astype(jnp.float32)
            pre_t[rows, :] = pre_gradient(et[rows, :], ft[rows, :], grad)

    def own_images():
        for c in range(2):
            rows = pl.ds(c * (n // 2), n // 2)
            total = acc_i[rows, :] + mm(w[0, 1, rows, :], tp[...])
            grad = logit_scale * total - logit_scale * tm[rows, :].astype(jnp.float32)
            pre_i[rows, :] = pre_gradient(ei[rows, :], fi[rows, :], grad)


    def added(p, q):
        return (p.astype(jnp.float32) + q.astype(jnp.float32)).astype(jnp.bfloat16)

    ij = ((x, y), (y, x))
    pi, pj = (px, py), (py, px)
    both = range(2)

    def head_half(which, dst, flipped, pre, first, z_first):
        part, eh = dst.shape[4:]
        half = flipped.shape[0] // 2
        rows = pl.ds(pl.multiple_of(which * half, half), half)
        g = mm(flipped[rows, :], pre[:, pl.ds(first, 2 * eh)])
        for q in range(4):
            for ab in both:
                for k in range(nz):
                    row = (q * nz + k) * part
                    piece = g[row : row + part, ab * eh : (ab + 1) * eh].astype(jnp.bfloat16)
                    if z_first:
                        dst[k, ab, q // 2, q % 2] = piece
                    else:
                        dst[ab, q // 2, q % 2, k] = piece

    def widen(cc, full, result, first_column, z_first):
        part, eh = full.shape[5:]
        for ab in both:
            for q in range(4):
                for k in range(nz):
                    first = pl.multiple_of(((cc * 4 + q) * nz + k) * part, part)
                    where = (k, ab, q // 2, q % 2) if z_first else (ab, q // 2, q % 2, k)
                    result[pl.ds(first, part), pl.ds(first_column + ab * eh, eh)] = full[
                        (cc, *where)
                    ].astype(jnp.float32)

    def reduce_z_first(flipped, pre, result, first_column, bufs):
        out_half, own, from_core, rz, r1, r2, full = bufs
        place = [lax.rem(z + k, nz) for k in range(nz)]
        head_half(1 - core, out_half, flipped, pre, first_column, True)
        got = [push(out_half.at[place[k]], from_core.at[place[k]], pc) for k in [*range(1, nz), 0]]
        got = got[-1:] + got[:-1]
        head_half(core, own, flipped, pre, first_column, True)
        yield
        sz = []
        for k in range(1, nz):
            got[k].wait_recv()
            own[place[k]] = added(own[place[k]], from_core[place[k]])
            sz.append(push(own.at[place[k]], rz.at[k], pz[k - 1]))
        got[0].wait_recv()
        total = own[z].astype(jnp.float32) + from_core[z].astype(jnp.float32)
        yield
        for k in range(1, nz):
            sz[k - 1].wait_recv()
            total = total + rz[k].astype(jnp.float32)
        own[z] = total.astype(jnp.bfloat16)
        s1 = [push(own.at[z, ab, 1 - ij[ab][0]], r1.at[ab], pi[ab]) for ab in both]
        yield
        s2 = []
        for ab in both:
            i, j = ij[ab]
            s1[ab].wait_recv()
            own[z, ab, i] = added(own[z, ab, i], r1[ab])
            s2.append(push(own.at[z, ab, i, 1 - j], r2.at[ab], pj[ab]))
        yield
        s3 = []
        for ab in both:
            i, j = ij[ab]
            s2[ab].wait_recv()
            full[core, z, ab, i, j] = added(own[z, ab, i, j], r2[ab])
            piece = full.at[core, z, ab, i, j]
            s3.append(push(piece, piece, pj[ab]))
        yield
        s4 = []
        for ab in both:
            s3[ab].wait_recv()
            piece = full.at[core, z, ab, ij[ab][0]]
            s4.append(push(piece, piece, pi[ab]))
        yield
        for ab in both:
            s4[ab].wait_recv()
        piece = full.at[core, z]
        s5 = [push(piece, piece, pz[k - 1]) for k in range(1, nz)]
        last = [push(piece, piece, pc)]
        yield
        for k in range(1, nz):
            s5[k - 1].wait_recv()
            piece = full.at[core, lax.rem(z + nz - k, nz)]
            last.append(push(piece, piece, pc))
        widen(core, full, result, first_column, True)
        yield
        for copy in last:
            copy.wait_recv()
        widen(1 - core, full, result, first_column, True)
        yield

    def reduce_head(flipped, pre, result, first_column, bufs):
        out_half, own, from_core, r1, r2, r3, full = bufs
        head_half(1 - core, out_half, flipped, pre, first_column, False)
        first, second = [
            [push(out_half.at[ab, i], from_core.at[ab, i], pc) for ab, i in places]
            for places in (
                [(ab, 1 - ij[ab][0]) for ab in both],
                [(ab, ij[ab][0]) for ab in both],
            )
        ]
        head_half(core, own, flipped, pre, first_column, False)
        yield
        s1 = []
        for ab in both:
            i = ij[ab][0]
            first[ab].wait_recv()
            own[ab, 1 - i] = added(own[ab, 1 - i], from_core[ab, 1 - i])
            s1.append(push(own.at[ab, 1 - i], r1.at[ab], pi[ab]))
        for ab in both:
            i = ij[ab][0]
            second[ab].wait_recv()
            own[ab, i] = added(own[ab, i], from_core[ab, i])
        yield
        s2 = []
        for ab in both:
            i, j = ij[ab]
            s1[ab].wait_recv()
            own[ab, i] = added(own[ab, i], r1[ab])
            s2.append(push(own.at[ab, i, 1 - j], r2.at[ab], pj[ab]))
        yield
        s3 = []
        for ab in both:
            i, j = ij[ab]
            s2[ab].wait_recv()
            own[ab, i, j] = added(own[ab, i, j], r2[ab])
            s3.append(
                [push(own.at[ab, i, j, lax.rem(z + k, nz)], r3.at[ab, k], pz[k - 1]) for k in range(1, nz)]
            )
        yield
        s4 = []
        for ab in both:
            i, j = ij[ab]
            total = own[ab, i, j, z].astype(jnp.float32)
            for k in range(1, nz):
                s3[ab][k - 1].wait_recv()
                total = total + r3[ab, k].astype(jnp.float32)
            full[core, ab, i, j, z] = total.astype(jnp.bfloat16)
            piece = full.at[core, ab, i, j, z]
            s4.append([push(piece, piece, pz[k - 1]) for k in range(1, nz)])
        yield
        s5 = []
        for ab in both:
            i, j = ij[ab]
            for copy in s4[ab]:
                copy.wait_recv()
            piece = full.at[core, ab, i, j]
            s5.append(push(piece, piece, pj[ab]))
        yield
        s6, last = [], []
        for ab in both:
            i, j = ij[ab]
            s5[ab].wait_recv()
            piece = full.at[core, ab, i]
            s6.append(push(piece, piece, pi[ab]))
            last.append(push(piece, piece, pc))
        yield
        for ab in both:
            i, j = ij[ab]
            s6[ab].wait_recv()
            piece = full.at[core, ab, 1 - i]
            last.append(push(piece, piece, pc))
        widen(core, full, result, first_column, False)
        yield
        for copy in last:
            copy.wait_recv()
        widen(1 - core, full, result, first_column, False)
        yield

    def back(head, c):
        rows = pl.ds(c * chunk, chunk)
        sums[head, c].wait_recv()
        if head == "t":
            back_t[rows, :] = mm(added(pre_t[rows, :], got_pre_t[rows, :]), wt[...], NT)
        else:
            back_i[rows, :] = mm(added(pre_i[rows, :], got_pre_i[rows, :]), wi[...], NT)

    chains = {}
    for head, kinds, flipped, pre, result, parts in (
        ("t", KINDS_T, xtt, pre_t, ht, bufs_t),
        ("i", KINDS_I, xit, pre_i, hi, bufs_i),
    ):
        for k, kind in enumerate(kinds):
            reduce = reduce_z_first if kind == "z" else reduce_head
            chains[head, k] = reduce(flipped, pre, result, k * (e // len(kinds)), parts[k])
    for what, head, k in ORDER:
        if what == "near":
            texts_of_neighbour(k) if head == "t" else images_of_neighbour(k)
        elif what == "own":
            own_texts() if head == "t" else own_images()
        elif what == "send":
            send_sum(head, k)
        elif what == "back":
            back(head, k)
        else:
            next(chains[head, k])
    for copy in started:
        copy.wait_send()


def tail(bi, bt, hi, ht, bi_out, bt_out, hi_out, ht_out, sems):
    copies = [
        pltpu.make_async_copy(src, dst, sems.at[k])
        for k, (src, dst) in enumerate(
            ((bi, bi_out), (bt, bt_out), (hi, hi_out), (ht, ht_out))
        )
    ]
    for copy in copies:
        copy.start()
    for copy in copies:
        copy.wait()


def kernel_shards(nz, image_feats, text_feats, image_head, text_head, image_lse, text_lse):
    n, di = image_feats.shape[1:]
    dt, e = text_head.shape
    chunk = n // 4
    bf, f32 = jnp.bfloat16, jnp.float32
    vm = pltpu.VMEM

    def buffers(rows, kinds):
        piece = (rows // (8 * nz), e // len(kinds) // 2)
        x_first = [(2, 2, 2, nz)] * 3 + [(2, 2, nz), (2, nz), (2, nz), (2, 2, 2, 2, nz)]
        z_first = [(nz, 2, 2, 2)] * 4 + [(2, 2), (2,), (2, nz, 2, 2, 2)]
        return [
            [vm((*lead, *piece), bf) for lead in (z_first if kind == "z" else x_first)]
            for kind in kinds
        ]

    copies = 2 + 4 * (n // chunk) + len(KINDS_I + KINDS_T) * (4 + 2 + 2 + 2 * (nz - 1) * 2 + 2 + 2 + 4)
    spec = pl.BlockSpec(memory_space=pltpu.VMEM)
    anywhere = pl.BlockSpec(memory_space=pl.ANY)
    image_back, text_back, image_total, text_total = pl.pallas_call(
        functools.partial(fused, nz, chunk),
        out_shape=[vm((n, di), f32), vm((n, dt), f32), vm((di, e), f32), vm((dt, e), f32)],
        in_specs=[anywhere] * 4 + [spec] * 2,
        out_specs=[spec] * 4,
        scratch_shapes=[
            vm((n, di), bf), vm((n, dt), bf), vm((n, di), bf), vm((n, dt), bf),
            vm((di, e), bf), vm((dt, e), bf),
            vm((2 * n, e), bf), vm((2 * n, e), bf), vm((n, e), bf), vm((n, e), bf),
            vm((n, e), f32), vm((n, e), f32), vm((n, e), f32), vm((n, e), f32),
            vm((n, 1), f32), vm((n, 1), f32), vm((n, 1), f32), vm((n, 1), f32),
            vm((n, e), bf), vm((n, e), bf), vm((n, e), bf), vm((n, e), bf),
            vm((1, n), f32), vm((1, n), f32), vm((2, n, 128), f32), vm((2, 1, n), f32),
            vm((2, 2, n, n), bf),
            vm((n, e), f32), vm((n, e), f32), vm((n, e), f32), vm((n, e), f32),
            vm((di, 2 * n), bf), vm((dt, 2 * n), bf),
            buffers(di, KINDS_I), buffers(dt, KINDS_T),
            pltpu.SemaphoreType.DMA((copies,)), pltpu.SemaphoreType.DMA((copies,)),
            pltpu.SemaphoreType.DMA((4,)),
        ],
        compiler_params=pltpu.CompilerParams(
            collective_id=0, has_side_effects=True, vmem_limit_bytes=54 * 1024 * 1024
        ),
    )(image_feats[0], text_feats[0], image_head, text_head, image_lse, text_lse)
    shapes = [(n, di), (n, dt), (di, e), (dt, e)]
    image_back, text_back, image_total, text_total = pl.pallas_call(
        tail,
        out_shape=[jax.ShapeDtypeStruct(shape, f32) for shape in shapes],
        in_specs=[spec] * 4,
        out_specs=[anywhere] * 4,
        scratch_shapes=[pltpu.SemaphoreType.DMA((4,))],
        compiler_params=pltpu.CompilerParams(vmem_limit_bytes=4 * 1024 * 1024),
    )(image_back, text_back, image_total, text_total)
    return (image_back[None], text_back[None], image_total, text_total)


def solution(mesh):
    blk, rep = mesh.shape["blk"], mesh.shape["rep"]
    body = shards
    if blk == SIDE * SIDE and rep % SIDE == 0:
        body = functools.partial(kernel_shards, rep // SIDE)
    return jax.shard_map(
        body,
        mesh=mesh,
        in_specs=(
            P("rep", "blk", None),
            P("rep", "blk", None),
            P(),
            P(),
            P("rep", "blk"),
            P("rep", "blk"),
        ),
        out_specs=(P("rep", "blk", None), P("rep", "blk", None), P(), P()),
        check_vma=False,
    )
```

```python
import functools

import jax
import jax.numpy as jnp
from jax import lax
from jax.experimental import pallas as pl
from jax.experimental.pallas import tpu as pltpu
from jax.sharding import PartitionSpec as P

logit_scale = 50.0
epsilon = 1e-06


def project_head(feats, weight):
    raw = jnp.dot(feats, weight, preferred_element_type=jnp.float32)
    factor = lax.rsqrt(jnp.sum(raw * raw, axis=1, keepdims=True) + epsilon)
    return (raw * factor, factor)


def pre_gradient(embed, factor, grad):
    inner = jnp.sum(embed * grad, axis=1, keepdims=True)
    return (factor * (grad - embed * inner)).astype(jnp.bfloat16)


def weight_tile(left, left_lse, right, right_lse):
    scores = logit_scale * lax.dot_general(
        left, right, (((1,), (1,)), ((), ())), preferred_element_type=jnp.float32
    )
    return (
        0.5 * (jnp.exp(scores - left_lse[:, None]) + jnp.exp(scores - right_lse[None, :]))
    ).astype(jnp.bfloat16)


def shards(image_feats, text_feats, image_head, text_head, image_lse, text_lse):
    image_rows = image_feats[0]
    text_rows = text_feats[0]
    lse_img = image_lse[0]
    lse_txt = text_lse[0]
    image_embed, image_scale = project_head(image_rows, image_head)
    text_embed, text_scale = project_head(text_rows, text_head)
    image_round = image_embed.astype(jnp.bfloat16)
    text_round = text_embed.astype(jnp.bfloat16)
    image_piece = lax.all_gather(image_round, "blk", axis=0, tiled=True)
    image_piece_lse = lax.all_gather(
        lse_img.astype(jnp.bfloat16), "blk", axis=0, tiled=True
    ).astype(jnp.float32)
    text_piece = lax.all_gather(text_round, "blk", axis=0, tiled=True)
    text_piece_lse = lax.all_gather(lse_txt.astype(jnp.bfloat16), "blk", axis=0, tiled=True).astype(
        jnp.float32
    )
    image_weights = weight_tile(image_round, lse_img, text_piece, text_piece_lse)
    image_total_part = jnp.dot(image_weights, text_piece, preferred_element_type=jnp.float32)
    text_weights = weight_tile(image_piece, image_piece_lse, text_round, lse_txt)
    text_total_part = lax.dot_general(
        text_weights, image_piece, (((0,), (0,)), ((), ())), preferred_element_type=jnp.float32
    )
    image_grad = logit_scale * image_total_part - logit_scale * text_round.astype(jnp.float32)
    text_grad = logit_scale * text_total_part - logit_scale * image_round.astype(jnp.float32)
    image_pre = pre_gradient(image_embed, image_scale, image_grad)
    text_pre = pre_gradient(text_embed, text_scale, text_grad)
    image_back = lax.dot_general(
        image_pre, image_head, (((1,), (1,)), ((), ())), preferred_element_type=jnp.float32
    )
    text_back = lax.dot_general(
        text_pre, text_head, (((1,), (1,)), ((), ())), preferred_element_type=jnp.float32
    )
    image_wgrad = lax.dot_general(
        image_rows, image_pre, (((0,), (0,)), ((), ())), preferred_element_type=jnp.float32
    )
    text_wgrad = lax.dot_general(
        text_rows, text_pre, (((0,), (0,)), ((), ())), preferred_element_type=jnp.float32
    )
    image_total, text_total = lax.psum((image_wgrad, text_wgrad), ("blk", "rep"))
    return (image_back[None], text_back[None], image_total, text_total)


MESH = pl.DeviceIdType.MESH
SIDE = 2
KINDS_I, KINDS_T = "nzn", "nnn"
ORDER = (
    ("near", "t", 0),
    ("send", "t", 0),
    ("step", "i", 1),
    ("step", "i", 0),
    ("own", "t", 0),
    ("step", "i", 1),
    ("near", "t", 1),
    ("step", "i", 0),
    ("step", "t", 2),
    ("step", "i", 2),
    ("step", "t", 2),
    ("step", "t", 1),
    ("step", "i", 2),
    ("step", "t", 0),
    ("step", "t", 1),
    ("step", "i", 0),
    ("step", "t", 0),
    ("step", "i", 2),
    ("step", "i", 1),
    ("step", "t", 1),
    ("step", "t", 2),
    ("step", "i", 0),
    ("send", "t", 2),
    ("step", "i", 2),
    ("step", "i", 1),
    ("step", "t", 0),
    ("step", "t", 1),
    ("send", "t", 1),
    ("step", "t", 2),
    ("step", "i", 0),
    ("step", "i", 1),
    ("step", "i", 2),
    ("step", "t", 0),
    ("back", "t", 0),
    ("step", "t", 2),
    ("step", "t", 1),
    ("send", "t", 3),
    ("step", "i", 2),
    ("step", "i", 1),
    ("step", "i", 0),
    ("step", "t", 0),
    ("step", "t", 2),
    ("back", "i", 2),
    ("back", "i", 1),
    ("step", "t", 1),
    ("back", "i", 3),
    ("step", "i", 2),
    ("step", "i", 1),
    ("step", "t", 0),
    ("step", "i", 0),
    ("step", "t", 1),
    ("step", "t", 2),
    ("back", "i", 0),
    ("back", "t", 2),
    ("step", "i", 2),
    ("back", "t", 3),
    ("step", "t", 0),
    ("step", "i", 2),
    ("step", "i", 0),
    ("step", "t", 1),
    ("back", "t", 1),
    ("step", "t", 2),
    ("step", "i", 1),
    ("step", "t", 0),
    ("step", "t", 2),
    ("step", "i", 0),
    ("step", "t", 1),
    ("step", "i", 1),
    ("step", "t", 0),
)
NT = (((1,), (1,)), ((), ()))
TN = (((0,), (0,)), ((), ()))


def mm(a, b, dims=(((1,), (0,)), ((), ()))):
    return lax.dot_general(a, b, dims, preferred_element_type=jnp.float32)


def fused(
    nz, chunk,
    xi_in, xt_in, wi_in, wt_in, li, lt,
    back_i, back_t, hi, ht,
    xi, xt, xin, xtn, wi, wt, pre_i, pre_t, got_pre_i, got_pre_t,
    ei, et, ein, etn, fi, ft, fin, ftn,
    im, ip, tm, tp, lip, ltp, u, v, w,
    acc_i, acc_t, acc_tn, xit, xtt,
    bufs_i, bufs_t,
    send, recv, local,
):
    n, e = im.shape
    di, dt = wi.shape[0], wt.shape[0]
    count = n // chunk
    b, r = lax.axis_index("blk"), lax.axis_index("rep")
    x, y = lax.rem(b, 2), b // 2
    core, z = lax.rem(r, 2), r // 2
    px = {"blk": y * 2 + 1 - x, "rep": r}
    py = {"blk": (1 - y) * 2 + x, "rep": r}
    pc = {"blk": b, "rep": z * 2 + 1 - core}
    pz = [{"blk": b, "rep": lax.rem(z + k, nz) * 2 + core} for k in range(1, nz)]
    along_x, along_y = y * 2 + 1 - x, (1 - y) * 2 + x
    p_img = {"blk": along_x * (1 - core) + along_y * core, "rep": r}
    p_txt = {"blk": along_y * (1 - core) + along_x * core, "rep": r}

    used = [0]

    def push(src, dst, dev):
        s = used[0]
        used[0] += 1
        copy = pltpu.make_async_remote_copy(
            src_ref=src, dst_ref=dst, send_sem=send.at[s], recv_sem=recv.at[s],
            device_id=dev, device_id_type=MESH,
        )
        copy.start()
        started.append(copy)
        return copy

    started, moved = [], []

    def move(src, dst):
        copy = pltpu.make_async_copy(src, dst, local.at[len(moved)])
        copy.start()
        moved.append(copy)
        return copy

    barrier = pltpu.get_barrier_semaphore()
    for dev in [px, py, pc] + pz:
        pl.semaphore_signal(barrier, inc=1, device_id=dev, device_id_type=MESH)
    loads = [move(wi_in, wi), move(xi_in, xi), move(wt_in, wt), move(xt_in, xt)]
    pl.semaphore_wait(barrier, 2 + nz)
    block = n // 2
    early, late = pl.ds(0, block), pl.ds(block, block)
    arrivals = ((0, block), (block, chunk), (block + chunk, chunk))
    got_li = push(li, lip, p_img)
    got_lt = push(lt, ltp, p_txt)
    got_t = [push(xt_in.at[rows, :], xtn.at[rows, :], p_txt) for rows in (early, late)]
    got_i = [push(xi_in.at[early, :], xin.at[early, :], p_img)]

    def project(rows, feats, head, embed, factor, rounded):
        raw = mm(feats[rows, :], head[...])
        f = lax.rsqrt(jnp.sum(raw * raw, axis=1, keepdims=True) + epsilon)
        out = raw * f
        embed[rows, :] = out
        factor[rows, :] = f
        rounded[rows, :] = out.astype(jnp.bfloat16)

    for copy in loads[:2]:
        copy.wait()

    @pl.loop(0, count)
    def _(c):
        project(pl.ds(pl.multiple_of(c * chunk, chunk), chunk), xi, wi, ei, fi, im)

    for copy in loads[2:]:
        copy.wait()

    @pl.loop(0, count)
    def _(c):
        project(pl.ds(pl.multiple_of(c * chunk, chunk), chunk), xt, wt, et, ft, tm)

    def columns(lse):
        half = 0.5 * jnp.exp(-lse)
        return jnp.transpose(jnp.broadcast_to(half, (128, n)))

    u[0] = columns(li[...])
    v[0] = 0.5 * jnp.exp(-lt[...])
    images, texts = (im, ip), (tm, tp)

    def tile(p, q, r0, nr, c0, nc):
        s = logit_scale * mm(images[p][pl.ds(r0, nr), :], texts[q][pl.ds(c0, nc), :], NT)
        fac = u[p, pl.ds(r0, nr), :][:, :1] + v[q, :, pl.ds(c0, nc)]
        w[p, q, pl.ds(r0, nr), pl.ds(c0, nc)] = (jnp.exp(s) * fac).astype(jnp.bfloat16)

    @pl.loop(0, count)
    def _(c):
        tile(0, 0, pl.multiple_of(c * chunk, chunk), chunk, 0, n)

    @pl.loop(0, count)
    def _(c):
        rows = pl.ds(pl.multiple_of(c * chunk, chunk), chunk)
        acc_i[rows, :] = mm(w[0, 0, rows, :], tm[...])
        acc_t[rows, :] = mm(w[0, 0, :, rows], im[...], TN)

    for src, dst, width in ((xi, xit, di), (xt, xtt, dt)):

        @pl.loop(0, width // 128)
        def _(k, src=src, dst=dst):
            part = pl.ds(pl.multiple_of(k * 128, 128), 128)
            dst[part, pl.ds(0, n)] = jnp.transpose(src[:, part])

    got_li.wait_recv()
    got_lt.wait_recv()
    u[1] = columns(lip[...])
    v[1] = 0.5 * jnp.exp(-ltp[...])
    for c in range(2):
        rows = pl.ds(c * block, block)
        got_t[c].wait_recv()
        if c == 1:
            for first, size in arrivals[1:]:
                part = pl.ds(first, size)
                got_i.append(push(xi_in.at[part, :], xin.at[part, :], p_img))
        project(rows, xtn, wt, etn, ftn, tp)
        tile(0, 1, 0, n, c * block, block)
        acc_tn[rows, :] = mm(w[0, 1, :, rows], im[...], TN)
        xtt[:, pl.ds(n + c * block, block)] = jnp.transpose(xtn[rows, :])

    sums = {}

    def texts_of_neighbour(c):
        rows, later = pl.ds(c * block, block), pl.ds(n + c * block, block)
        total = acc_tn[rows, :] + mm(w[1, 1, late, rows], ip[late, :], TN)
        pre_t[later, :] = pre_gradient(etn[rows, :], ftn[rows, :], logit_scale * total)

    def send_sum(head, c):
        rows, later = pl.ds(c * chunk, chunk), pl.ds(n + c * chunk, chunk)
        if head == "t":
            sums[head, c] = push(pre_t.at[later, :], got_pre_t.at[rows, :], p_txt)
        else:
            sums[head, c] = push(pre_i.at[later, :], got_pre_i.at[rows, :], p_img)

    def own_texts():
        for c in range(2):
            rows = pl.ds(c * (n // 2), n // 2)
            total = acc_t[rows, :] + mm(w[1, 0, late, rows], ip[late, :], TN)
            grad = logit_scale * total - logit_scale * im[rows, :].astype(jnp.float32)
            pre_t[rows, :] = pre_gradient(et[rows, :], ft[rows, :], grad)

    def own_images():
        for c in range(2):
            rows = pl.ds(c * (n // 2), n // 2)
            total = acc_i[rows, :] + mm(w[0, 1, rows, :], tp[...])
            grad = logit_scale * total - logit_scale * tm[rows, :].astype(jnp.float32)
            pre_i[rows, :] = pre_gradient(ei[rows, :], fi[rows, :], grad)


    own_images()
    for c, (first, size) in enumerate(arrivals):
        rows, later = pl.ds(first, size), pl.ds(n + first, size)
        got_i[c].wait_recv()
        project(rows, xin, wi, ein, fin, ip)
        tile(1, 0, first, size, 0, n)
        tile(1, 1, first, size, 0, n)
        total = mm(w[1, 0, rows, :], tm[...]) + mm(w[1, 1, rows, :], tp[...])
        pre_i[later, :] = pre_gradient(ein[rows, :], fin[rows, :], logit_scale * total)
        for k in range(first // chunk, (first + size) // chunk):
            send_sum("i", k)
        xit[:, later] = jnp.transpose(xin[rows, :])
        if c == 0:
            acc_t[...] += mm(w[1, 0, early, :], ip[early, :], TN)
            acc_tn[...] += mm(w[1, 1, early, :], ip[early, :], TN)

    def added(p, q):
        return (p.astype(jnp.float32) + q.astype(jnp.float32)).astype(jnp.bfloat16)

    ij = ((x, y), (y, x))
    pi, pj = (px, py), (py, px)
    both = range(2)

    def head_half(which, dst, flipped, pre, first, z_first):
        part, eh = dst.shape[4:]
        half = flipped.shape[0] // 2
        rows = pl.ds(pl.multiple_of(which * half, half), half)
        g = mm(flipped[rows, :], pre[:, pl.ds(first, 2 * eh)])
        for q in range(4):
            for ab in both:
                for k in range(nz):
                    row = (q * nz + k) * part
                    piece = g[row : row + part, ab * eh : (ab + 1) * eh].astype(jnp.bfloat16)
                    if z_first:
                        dst[k, ab, q // 2, q % 2] = piece
                    else:
                        dst[ab, q // 2, q % 2, k] = piece

    def widen(cc, full, result, first_column, z_first):
        part, eh = full.shape[5:]
        for ab in both:
            for q in range(4):
                for k in range(nz):
                    first = pl.multiple_of(((cc * 4 + q) * nz + k) * part, part)
                    where = (k, ab, q // 2, q % 2) if z_first else (ab, q // 2, q % 2, k)
                    result[pl.ds(first, part), pl.ds(first_column + ab * eh, eh)] = full[
                        (cc, *where)
                    ].astype(jnp.float32)

    def reduce_z_first(flipped, pre, result, first_column, bufs):
        out_half, own, from_core, rz, r1, r2, full = bufs
        place = [lax.rem(z + k, nz) for k in range(nz)]
        head_half(1 - core, out_half, flipped, pre, first_column, True)
        got = [push(out_half.at[place[k]], from_core.at[place[k]], pc) for k in [*range(1, nz), 0]]
        got = got[-1:] + got[:-1]
        head_half(core, own, flipped, pre, first_column, True)
        yield
        sz = []
        for k in range(1, nz):
            got[k].wait_recv()
            own[place[k]] = added(own[place[k]], from_core[place[k]])
            sz.append(push(own.at[place[k]], rz.at[k], pz[k - 1]))
        got[0].wait_recv()
        total = own[z].astype(jnp.float32) + from_core[z].astype(jnp.float32)
        yield
        for k in range(1, nz):
            sz[k - 1].wait_recv()
            total = total + rz[k].astype(jnp.float32)
        own[z] = total.astype(jnp.bfloat16)
        s1 = [push(own.at[z, ab, 1 - ij[ab][0]], r1.at[ab], pi[ab]) for ab in both]
        yield
        s2 = []
        for ab in both:
            i, j = ij[ab]
            s1[ab].wait_recv()
            own[z, ab, i] = added(own[z, ab, i], r1[ab])
            s2.append(push(own.at[z, ab, i, 1 - j], r2.at[ab], pj[ab]))
        yield
        s3 = []
        for ab in both:
            i, j = ij[ab]
            s2[ab].wait_recv()
            full[core, z, ab, i, j] = added(own[z, ab, i, j], r2[ab])
            piece = full.at[core, z, ab, i, j]
            s3.append(push(piece, piece, pj[ab]))
        yield
        s4 = []
        for ab in both:
            s3[ab].wait_recv()
            piece = full.at[core, z, ab, ij[ab][0]]
            s4.append(push(piece, piece, pi[ab]))
        yield
        for ab in both:
            s4[ab].wait_recv()
        piece = full.at[core, z]
        s5 = [push(piece, piece, pz[k - 1]) for k in range(1, nz)]
        last = [push(piece, piece, pc)]
        yield
        for k in range(1, nz):
            s5[k - 1].wait_recv()
            piece = full.at[core, lax.rem(z + nz - k, nz)]
            last.append(push(piece, piece, pc))
        widen(core, full, result, first_column, True)
        yield
        for copy in last:
            copy.wait_recv()
        widen(1 - core, full, result, first_column, True)
        yield

    def reduce_head(flipped, pre, result, first_column, bufs):
        out_half, own, from_core, r1, r2, r3, full = bufs
        head_half(1 - core, out_half, flipped, pre, first_column, False)
        first, second = [
            [push(out_half.at[ab, i], from_core.at[ab, i], pc) for ab, i in places]
            for places in (
                [(ab, 1 - ij[ab][0]) for ab in both],
                [(ab, ij[ab][0]) for ab in both],
            )
        ]
        head_half(core, own, flipped, pre, first_column, False)
        yield
        s1 = []
        for ab in both:
            i = ij[ab][0]
            first[ab].wait_recv()
            own[ab, 1 - i] = added(own[ab, 1 - i], from_core[ab, 1 - i])
            s1.append(push(own.at[ab, 1 - i], r1.at[ab], pi[ab]))
        for ab in both:
            i = ij[ab][0]
            second[ab].wait_recv()
            own[ab, i] = added(own[ab, i], from_core[ab, i])
        yield
        s2 = []
        for ab in both:
            i, j = ij[ab]
            s1[ab].wait_recv()
            own[ab, i] = added(own[ab, i], r1[ab])
            s2.append(push(own.at[ab, i, 1 - j], r2.at[ab], pj[ab]))
        yield
        s3 = []
        for ab in both:
            i, j = ij[ab]
            s2[ab].wait_recv()
            own[ab, i, j] = added(own[ab, i, j], r2[ab])
            s3.append(
                [push(own.at[ab, i, j, lax.rem(z + k, nz)], r3.at[ab, k], pz[k - 1]) for k in range(1, nz)]
            )
        yield
        s4 = []
        for ab in both:
            i, j = ij[ab]
            total = own[ab, i, j, z].astype(jnp.float32)
            for k in range(1, nz):
                s3[ab][k - 1].wait_recv()
                total = total + r3[ab, k].astype(jnp.float32)
            full[core, ab, i, j, z] = total.astype(jnp.bfloat16)
            piece = full.at[core, ab, i, j, z]
            s4.append([push(piece, piece, pz[k - 1]) for k in range(1, nz)])
        yield
        s5 = []
        for ab in both:
            i, j = ij[ab]
            for copy in s4[ab]:
                copy.wait_recv()
            piece = full.at[core, ab, i, j]
            s5.append(push(piece, piece, pj[ab]))
        yield
        s6, last = [], []
        for ab in both:
            i, j = ij[ab]
            s5[ab].wait_recv()
            piece = full.at[core, ab, i]
            s6.append(push(piece, piece, pi[ab]))
            last.append(push(piece, piece, pc))
        yield
        for ab in both:
            i, j = ij[ab]
            s6[ab].wait_recv()
            piece = full.at[core, ab, 1 - i]
            last.append(push(piece, piece, pc))
        widen(core, full, result, first_column, False)
        yield
        for copy in last:
            copy.wait_recv()
        widen(1 - core, full, result, first_column, False)
        yield

    def back(head, c):
        rows = pl.ds(c * chunk, chunk)
        sums[head, c].wait_recv()
        if head == "t":
            back_t[rows, :] = mm(added(pre_t[rows, :], got_pre_t[rows, :]), wt[...], NT)
        else:
            back_i[rows, :] = mm(added(pre_i[rows, :], got_pre_i[rows, :]), wi[...], NT)

    chains = {}
    for head, kinds, flipped, pre, result, parts in (
        ("t", KINDS_T, xtt, pre_t, ht, bufs_t),
        ("i", KINDS_I, xit, pre_i, hi, bufs_i),
    ):
        for k, kind in enumerate(kinds):
            reduce = reduce_z_first if kind == "z" else reduce_head
            chains[head, k] = reduce(flipped, pre, result, k * (e // len(kinds)), parts[k])
    for what, head, k in ORDER:
        if what == "near":
            texts_of_neighbour(k)
        elif what == "own":
            own_texts()
        elif what == "send":
            send_sum(head, k)
        elif what == "back":
            back(head, k)
        else:
            next(chains[head, k])
    for copy in started:
        copy.wait_send()


def tail(bi, bt, hi, ht, bi_out, bt_out, hi_out, ht_out, sems):
    copies = [
        pltpu.make_async_copy(src, dst, sems.at[k])
        for k, (src, dst) in enumerate(
            ((bi, bi_out), (bt, bt_out), (hi, hi_out), (ht, ht_out))
        )
    ]
    for copy in copies:
        copy.start()
    for copy in copies:
        copy.wait()


def kernel_shards(nz, image_feats, text_feats, image_head, text_head, image_lse, text_lse):
    n, di = image_feats.shape[1:]
    dt, e = text_head.shape
    chunk = n // 4
    bf, f32 = jnp.bfloat16, jnp.float32
    vm = pltpu.VMEM

    def buffers(rows, kinds):
        piece = (rows // (8 * nz), e // len(kinds) // 2)
        x_first = [(2, 2, 2, nz)] * 3 + [(2, 2, nz), (2, nz), (2, nz), (2, 2, 2, 2, nz)]
        z_first = [(nz, 2, 2, 2)] * 4 + [(2, 2), (2,), (2, nz, 2, 2, 2)]
        return [
            [vm((*lead, *piece), bf) for lead in (z_first if kind == "z" else x_first)]
            for kind in kinds
        ]

    copies = 2 + 4 * (n // chunk) + len(KINDS_I + KINDS_T) * (4 + 2 + 2 + 2 * (nz - 1) * 2 + 2 + 2 + 4)
    spec = pl.BlockSpec(memory_space=pltpu.VMEM)
    anywhere = pl.BlockSpec(memory_space=pl.ANY)
    image_back, text_back, image_total, text_total = pl.pallas_call(
        functools.partial(fused, nz, chunk),
        out_shape=[vm((n, di), f32), vm((n, dt), f32), vm((di, e), f32), vm((dt, e), f32)],
        in_specs=[anywhere] * 4 + [spec] * 2,
        out_specs=[spec] * 4,
        scratch_shapes=[
            vm((n, di), bf), vm((n, dt), bf), vm((n, di), bf), vm((n, dt), bf),
            vm((di, e), bf), vm((dt, e), bf),
            vm((2 * n, e), bf), vm((2 * n, e), bf), vm((n, e), bf), vm((n, e), bf),
            vm((n, e), f32), vm((n, e), f32), vm((n, e), f32), vm((n, e), f32),
            vm((n, 1), f32), vm((n, 1), f32), vm((n, 1), f32), vm((n, 1), f32),
            vm((n, e), bf), vm((n, e), bf), vm((n, e), bf), vm((n, e), bf),
            vm((1, n), f32), vm((1, n), f32), vm((2, n, 128), f32), vm((2, 1, n), f32),
            vm((2, 2, n, n), bf),
            vm((n, e), f32), vm((n, e), f32), vm((n, e), f32),
            vm((di, 2 * n), bf), vm((dt, 2 * n), bf),
            buffers(di, KINDS_I), buffers(dt, KINDS_T),
            pltpu.SemaphoreType.DMA((copies,)), pltpu.SemaphoreType.DMA((copies,)),
            pltpu.SemaphoreType.DMA((4,)),
        ],
        compiler_params=pltpu.CompilerParams(
            collective_id=0, has_side_effects=True, vmem_limit_bytes=54 * 1024 * 1024
        ),
    )(image_feats[0], text_feats[0], image_head, text_head, image_lse, text_lse)
    shapes = [(n, di), (n, dt), (di, e), (dt, e)]
    image_back, text_back, image_total, text_total = pl.pallas_call(
        tail,
        out_shape=[jax.ShapeDtypeStruct(shape, f32) for shape in shapes],
        in_specs=[spec] * 4,
        out_specs=[anywhere] * 4,
        scratch_shapes=[pltpu.SemaphoreType.DMA((4,))],
        compiler_params=pltpu.CompilerParams(vmem_limit_bytes=4 * 1024 * 1024),
    )(image_back, text_back, image_total, text_total)
    return (image_back[None], text_back[None], image_total, text_total)


def solution(mesh):
    blk, rep = mesh.shape["blk"], mesh.shape["rep"]
    body = shards
    if blk == SIDE * SIDE and rep % SIDE == 0:
        body = functools.partial(kernel_shards, rep // SIDE)
    return jax.shard_map(
        body,
        mesh=mesh,
        in_specs=(
            P("rep", "blk", None),
            P("rep", "blk", None),
            P(),
            P(),
            P("rep", "blk"),
            P("rep", "blk"),
        ),
        out_specs=(P("rep", "blk", None), P("rep", "blk", None), P(), P()),
        check_vma=False,
    )
```

```python
import functools

import jax
import jax.numpy as jnp
from jax import lax
from jax.experimental import pallas as pl
from jax.experimental.pallas import tpu as pltpu
from jax.sharding import PartitionSpec as P

logit_scale = 50.0
epsilon = 1e-06


def project_head(feats, weight):
    raw = jnp.dot(feats, weight, preferred_element_type=jnp.float32)
    factor = lax.rsqrt(jnp.sum(raw * raw, axis=1, keepdims=True) + epsilon)
    return (raw * factor, factor)


def pre_gradient(embed, factor, grad):
    inner = jnp.sum(embed * grad, axis=1, keepdims=True)
    return (factor * (grad - embed * inner)).astype(jnp.bfloat16)


def weight_tile(left, left_lse, right, right_lse):
    scores = logit_scale * lax.dot_general(
        left, right, (((1,), (1,)), ((), ())), preferred_element_type=jnp.float32
    )
    return (
        0.5 * (jnp.exp(scores - left_lse[:, None]) + jnp.exp(scores - right_lse[None, :]))
    ).astype(jnp.bfloat16)


def shards(image_feats, text_feats, image_head, text_head, image_lse, text_lse):
    image_rows = image_feats[0]
    text_rows = text_feats[0]
    lse_img = image_lse[0]
    lse_txt = text_lse[0]
    image_embed, image_scale = project_head(image_rows, image_head)
    text_embed, text_scale = project_head(text_rows, text_head)
    image_round = image_embed.astype(jnp.bfloat16)
    text_round = text_embed.astype(jnp.bfloat16)
    image_piece = lax.all_gather(image_round, "blk", axis=0, tiled=True)
    image_piece_lse = lax.all_gather(
        lse_img.astype(jnp.bfloat16), "blk", axis=0, tiled=True
    ).astype(jnp.float32)
    text_piece = lax.all_gather(text_round, "blk", axis=0, tiled=True)
    text_piece_lse = lax.all_gather(lse_txt.astype(jnp.bfloat16), "blk", axis=0, tiled=True).astype(
        jnp.float32
    )
    image_weights = weight_tile(image_round, lse_img, text_piece, text_piece_lse)
    image_total_part = jnp.dot(image_weights, text_piece, preferred_element_type=jnp.float32)
    text_weights = weight_tile(image_piece, image_piece_lse, text_round, lse_txt)
    text_total_part = lax.dot_general(
        text_weights, image_piece, (((0,), (0,)), ((), ())), preferred_element_type=jnp.float32
    )
    image_grad = logit_scale * image_total_part - logit_scale * text_round.astype(jnp.float32)
    text_grad = logit_scale * text_total_part - logit_scale * image_round.astype(jnp.float32)
    image_pre = pre_gradient(image_embed, image_scale, image_grad)
    text_pre = pre_gradient(text_embed, text_scale, text_grad)
    image_back = lax.dot_general(
        image_pre, image_head, (((1,), (1,)), ((), ())), preferred_element_type=jnp.float32
    )
    text_back = lax.dot_general(
        text_pre, text_head, (((1,), (1,)), ((), ())), preferred_element_type=jnp.float32
    )
    image_wgrad = lax.dot_general(
        image_rows, image_pre, (((0,), (0,)), ((), ())), preferred_element_type=jnp.float32
    )
    text_wgrad = lax.dot_general(
        text_rows, text_pre, (((0,), (0,)), ((), ())), preferred_element_type=jnp.float32
    )
    image_total, text_total = lax.psum((image_wgrad, text_wgrad), ("blk", "rep"))
    return (image_back[None], text_back[None], image_total, text_total)


MESH = pl.DeviceIdType.MESH
SIDE = 2
KINDS_I, KINDS_T = "nzn", "nnn"
ORDER = (
    ("near", "t", 0),
    ("send", "t", 0),
    ("step", "i", 1),
    ("step", "i", 0),
    ("own", "t", 0),
    ("step", "i", 1),
    ("near", "t", 1),
    ("step", "i", 0),
    ("step", "t", 2),
    ("step", "i", 2),
    ("step", "t", 2),
    ("step", "t", 1),
    ("step", "i", 2),
    ("step", "t", 0),
    ("step", "t", 1),
    ("step", "i", 0),
    ("step", "t", 0),
    ("step", "i", 2),
    ("step", "i", 1),
    ("step", "t", 1),
    ("step", "t", 2),
    ("step", "i", 0),
    ("send", "t", 2),
    ("step", "i", 2),
    ("step", "i", 1),
    ("step", "t", 0),
    ("step", "t", 1),
    ("send", "t", 1),
    ("step", "t", 2),
    ("step", "i", 0),
    ("step", "i", 1),
    ("step", "i", 2),
    ("step", "t", 0),
    ("back", "t", 0),
    ("step", "t", 2),
    ("step", "t", 1),
    ("send", "t", 3),
    ("step", "i", 2),
    ("step", "i", 1),
    ("step", "i", 0),
    ("step", "t", 0),
    ("step", "t", 2),
    ("back", "i", 2),
    ("back", "i", 1),
    ("step", "t", 1),
    ("back", "i", 3),
    ("step", "i", 2),
    ("step", "i", 1),
    ("step", "t", 0),
    ("step", "i", 0),
    ("step", "t", 1),
    ("step", "t", 2),
    ("back", "i", 0),
    ("back", "t", 2),
    ("step", "i", 2),
    ("back", "t", 3),
    ("step", "t", 0),
    ("step", "i", 2),
    ("step", "i", 0),
    ("step", "t", 1),
    ("back", "t", 1),
    ("step", "t", 2),
    ("step", "i", 1),
    ("step", "t", 0),
    ("step", "t", 2),
    ("step", "i", 0),
    ("step", "t", 1),
    ("step", "i", 1),
    ("step", "t", 0),
)
NT = (((1,), (1,)), ((), ()))
TN = (((0,), (0,)), ((), ()))


def mm(a, b, dims=(((1,), (0,)), ((), ()))):
    return lax.dot_general(a, b, dims, preferred_element_type=jnp.float32)


def fused(
    nz, chunk,
    xi_in, xt_in, wi_in, wt_in, li, lt,
    back_i, back_t, hi, ht,
    xi, xt, xin, xtn, wi, wt, pre_i, pre_t, got_pre_i, got_pre_t,
    ei, et, ein, etn, fi, ft, fin, ftn,
    im, ip, tm, tp, lip, ltp, u, v, w,
    acc_i, acc_t, acc_tn, xit, xtt,
    bufs_i, bufs_t,
    send, recv, local,
):
    n, e = im.shape
    di, dt = wi.shape[0], wt.shape[0]
    count = n // chunk
    b, r = lax.axis_index("blk"), lax.axis_index("rep")
    x, y = lax.rem(b, 2), b // 2
    core, z = lax.rem(r, 2), r // 2
    px = {"blk": y * 2 + 1 - x, "rep": r}
    py = {"blk": (1 - y) * 2 + x, "rep": r}
    pc = {"blk": b, "rep": z * 2 + 1 - core}
    pz = [{"blk": b, "rep": lax.rem(z + k, nz) * 2 + core} for k in range(1, nz)]
    along_x, along_y = y * 2 + 1 - x, (1 - y) * 2 + x
    p_img = {"blk": along_x * (1 - core) + along_y * core, "rep": r}
    p_txt = {"blk": along_y * (1 - core) + along_x * core, "rep": r}

    used = [0]

    def push(src, dst, dev):
        s = used[0]
        used[0] += 1
        copy = pltpu.make_async_remote_copy(
            src_ref=src, dst_ref=dst, send_sem=send.at[s], recv_sem=recv.at[s],
            device_id=dev, device_id_type=MESH,
        )
        copy.start()
        started.append(copy)
        return copy

    started, moved = [], []

    def move(src, dst):
        copy = pltpu.make_async_copy(src, dst, local.at[len(moved)])
        copy.start()
        moved.append(copy)
        return copy

    barrier = pltpu.get_barrier_semaphore()
    for dev in [px, py, pc] + pz:
        pl.semaphore_signal(barrier, inc=1, device_id=dev, device_id_type=MESH)
    loads = [move(wi_in, wi), move(xi_in, xi), move(wt_in, wt), move(xt_in, xt)]
    pl.semaphore_wait(barrier, 2 + nz)
    block = n // 2
    early, late = pl.ds(0, block), pl.ds(block, block)
    arrivals = ((0, block), (block, chunk), (block + chunk, chunk))
    got_li = push(li, lip, p_img)
    got_lt = push(lt, ltp, p_txt)
    got_t = [push(xt_in.at[rows, :], xtn.at[rows, :], p_txt) for rows in (early, late)]
    got_i = []

    def project(rows, feats, head, embed, factor, rounded):
        raw = mm(feats[rows, :], head[...])
        f = lax.rsqrt(jnp.sum(raw * raw, axis=1, keepdims=True) + epsilon)
        out = raw * f
        embed[rows, :] = out
        factor[rows, :] = f
        rounded[rows, :] = out.astype(jnp.bfloat16)

    for copy in loads[:2]:
        copy.wait()

    @pl.loop(0, count)
    def _(c):
        project(pl.ds(pl.multiple_of(c * chunk, chunk), chunk), xi, wi, ei, fi, im)

    for copy in loads[2:]:
        copy.wait()

    @pl.loop(0, count)
    def _(c):
        project(pl.ds(pl.multiple_of(c * chunk, chunk), chunk), xt, wt, et, ft, tm)

    def columns(lse):
        half = 0.5 * jnp.exp(-lse)
        return jnp.transpose(jnp.broadcast_to(half, (128, n)))

    u[0] = columns(li[...])
    v[0] = 0.5 * jnp.exp(-lt[...])
    images, texts = (im, ip), (tm, tp)

    def tile(p, q, r0, nr, c0, nc):
        s = logit_scale * mm(images[p][pl.ds(r0, nr), :], texts[q][pl.ds(c0, nc), :], NT)
        fac = u[p, pl.ds(r0, nr), :][:, :1] + v[q, :, pl.ds(c0, nc)]
        w[p, q, pl.ds(r0, nr), pl.ds(c0, nc)] = (jnp.exp(s) * fac).astype(jnp.bfloat16)

    @pl.loop(0, count)
    def _(c):
        tile(0, 0, pl.multiple_of(c * chunk, chunk), chunk, 0, n)

    @pl.loop(0, count)
    def _(c):
        rows = pl.ds(pl.multiple_of(c * chunk, chunk), chunk)
        acc_i[rows, :] = mm(w[0, 0, rows, :], tm[...])
        acc_t[rows, :] = mm(w[0, 0, :, rows], im[...], TN)

    for src, dst, width in ((xi, xit, di), (xt, xtt, dt)):

        @pl.loop(0, width // 128)
        def _(k, src=src, dst=dst):
            part = pl.ds(pl.multiple_of(k * 128, 128), 128)
            dst[part, pl.ds(0, n)] = jnp.transpose(src[:, part])

    got_li.wait_recv()
    got_lt.wait_recv()
    u[1] = columns(lip[...])
    v[1] = 0.5 * jnp.exp(-ltp[...])
    for c in range(2):
        rows = pl.ds(c * block, block)
        got_t[c].wait_recv()
        for first, size in arrivals[:1] if c == 0 else arrivals[1:]:
            part = pl.ds(first, size)
            got_i.append(push(xi_in.at[part, :], xin.at[part, :], p_img))
        project(rows, xtn, wt, etn, ftn, tp)
        tile(0, 1, 0, n, c * block, block)
        acc_tn[rows, :] = mm(w[0, 1, :, rows], im[...], TN)
        xtt[:, pl.ds(n + c * block, block)] = jnp.transpose(xtn[rows, :])

    sums = {}

    def texts_of_neighbour(c):
        rows, later = pl.ds(c * block, block), pl.ds(n + c * block, block)
        total = acc_tn[rows, :] + mm(w[1, 1, late, rows], ip[late, :], TN)
        pre_t[later, :] = pre_gradient(etn[rows, :], ftn[rows, :], logit_scale * total)

    def send_sum(head, c):
        rows, later = pl.ds(c * chunk, chunk), pl.ds(n + c * chunk, chunk)
        if head == "t":
            sums[head, c] = push(pre_t.at[later, :], got_pre_t.at[rows, :], p_txt)
        else:
            sums[head, c] = push(pre_i.at[later, :], got_pre_i.at[rows, :], p_img)

    def own_texts():
        for c in range(2):
            rows = pl.ds(c * (n // 2), n // 2)
            total = acc_t[rows, :] + mm(w[1, 0, late, rows], ip[late, :], TN)
            grad = logit_scale * total - logit_scale * im[rows, :].astype(jnp.float32)
            pre_t[rows, :] = pre_gradient(et[rows, :], ft[rows, :], grad)

    def own_images():
        for c in range(2):
            rows = pl.ds(c * (n // 2), n // 2)
            total = acc_i[rows, :] + mm(w[0, 1, rows, :], tp[...])
            grad = logit_scale * total - logit_scale * tm[rows, :].astype(jnp.float32)
            pre_i[rows, :] = pre_gradient(ei[rows, :], fi[rows, :], grad)


    own_images()
    for c, (first, size) in enumerate(arrivals):
        rows, later = pl.ds(first, size), pl.ds(n + first, size)
        got_i[c].wait_recv()
        project(rows, xin, wi, ein, fin, ip)
        tile(1, 0, first, size, 0, n)
        tile(1, 1, first, size, 0, n)
        total = mm(w[1, 0, rows, :], tm[...]) + mm(w[1, 1, rows, :], tp[...])
        pre_i[later, :] = pre_gradient(ein[rows, :], fin[rows, :], logit_scale * total)
        for k in range(first // chunk, (first + size) // chunk):
            send_sum("i", k)
        xit[:, later] = jnp.transpose(xin[rows, :])
        if c == 0:
            acc_t[...] += mm(w[1, 0, early, :], ip[early, :], TN)
            acc_tn[...] += mm(w[1, 1, early, :], ip[early, :], TN)

    def added(p, q):
        return (p.astype(jnp.float32) + q.astype(jnp.float32)).astype(jnp.bfloat16)

    ij = ((x, y), (y, x))
    pi, pj = (px, py), (py, px)
    both = range(2)

    def head_half(which, dst, flipped, pre, first, z_first):
        part, eh = dst.shape[4:]
        half = flipped.shape[0] // 2
        rows = pl.ds(pl.multiple_of(which * half, half), half)
        g = mm(flipped[rows, :], pre[:, pl.ds(first, 2 * eh)])
        for q in range(4):
            for ab in both:
                for k in range(nz):
                    row = (q * nz + k) * part
                    piece = g[row : row + part, ab * eh : (ab + 1) * eh].astype(jnp.bfloat16)
                    if z_first:
                        dst[k, ab, q // 2, q % 2] = piece
                    else:
                        dst[ab, q // 2, q % 2, k] = piece

    def widen(cc, full, result, first_column, z_first):
        part, eh = full.shape[5:]
        for ab in both:
            for q in range(4):
                for k in range(nz):
                    first = pl.multiple_of(((cc * 4 + q) * nz + k) * part, part)
                    where = (k, ab, q // 2, q % 2) if z_first else (ab, q // 2, q % 2, k)
                    result[pl.ds(first, part), pl.ds(first_column + ab * eh, eh)] = full[
                        (cc, *where)
                    ].astype(jnp.float32)

    def reduce_z_first(flipped, pre, result, first_column, bufs):
        out_half, own, from_core, rz, r1, r2, full = bufs
        place = [lax.rem(z + k, nz) for k in range(nz)]
        head_half(1 - core, out_half, flipped, pre, first_column, True)
        got = [push(out_half.at[place[k]], from_core.at[place[k]], pc) for k in [*range(1, nz), 0]]
        got = got[-1:] + got[:-1]
        head_half(core, own, flipped, pre, first_column, True)
        yield
        sz = []
        for k in range(1, nz):
            got[k].wait_recv()
            own[place[k]] = added(own[place[k]], from_core[place[k]])
            sz.append(push(own.at[place[k]], rz.at[k], pz[k - 1]))
        got[0].wait_recv()
        total = own[z].astype(jnp.float32) + from_core[z].astype(jnp.float32)
        yield
        for k in range(1, nz):
            sz[k - 1].wait_recv()
            total = total + rz[k].astype(jnp.float32)
        own[z] = total.astype(jnp.bfloat16)
        s1 = [push(own.at[z, ab, 1 - ij[ab][0]], r1.at[ab], pi[ab]) for ab in both]
        yield
        s2 = []
        for ab in both:
            i, j = ij[ab]
            s1[ab].wait_recv()
            own[z, ab, i] = added(own[z, ab, i], r1[ab])
            s2.append(push(own.at[z, ab, i, 1 - j], r2.at[ab], pj[ab]))
        yield
        s3 = []
        for ab in both:
            i, j = ij[ab]
            s2[ab].wait_recv()
            full[core, z, ab, i, j] = added(own[z, ab, i, j], r2[ab])
            piece = full.at[core, z, ab, i, j]
            s3.append(push(piece, piece, pj[ab]))
        yield
        s4 = []
        for ab in both:
            s3[ab].wait_recv()
            piece = full.at[core, z, ab, ij[ab][0]]
            s4.append(push(piece, piece, pi[ab]))
        yield
        for ab in both:
            s4[ab].wait_recv()
        piece = full.at[core, z]
        s5 = [push(piece, piece, pz[k - 1]) for k in range(1, nz)]
        last = [push(piece, piece, pc)]
        yield
        for k in range(1, nz):
            s5[k - 1].wait_recv()
            piece = full.at[core, lax.rem(z + nz - k, nz)]
            last.append(push(piece, piece, pc))
        widen(core, full, result, first_column, True)
        yield
        for copy in last:
            copy.wait_recv()
        widen(1 - core, full, result, first_column, True)
        yield

    def reduce_head(flipped, pre, result, first_column, bufs):
        out_half, own, from_core, r1, r2, r3, full = bufs
        head_half(1 - core, out_half, flipped, pre, first_column, False)
        first, second = [
            [push(out_half.at[ab, i], from_core.at[ab, i], pc) for ab, i in places]
            for places in (
                [(ab, 1 - ij[ab][0]) for ab in both],
                [(ab, ij[ab][0]) for ab in both],
            )
        ]
        head_half(core, own, flipped, pre, first_column, False)
        yield
        s1 = []
        for ab in both:
            i = ij[ab][0]
            first[ab].wait_recv()
            own[ab, 1 - i] = added(own[ab, 1 - i], from_core[ab, 1 - i])
            s1.append(push(own.at[ab, 1 - i], r1.at[ab], pi[ab]))
        for ab in both:
            i = ij[ab][0]
            second[ab].wait_recv()
            own[ab, i] = added(own[ab, i], from_core[ab, i])
        yield
        s2 = []
        for ab in both:
            i, j = ij[ab]
            s1[ab].wait_recv()
            own[ab, i] = added(own[ab, i], r1[ab])
            s2.append(push(own.at[ab, i, 1 - j], r2.at[ab], pj[ab]))
        yield
        s3 = []
        for ab in both:
            i, j = ij[ab]
            s2[ab].wait_recv()
            own[ab, i, j] = added(own[ab, i, j], r2[ab])
            s3.append(
                [push(own.at[ab, i, j, lax.rem(z + k, nz)], r3.at[ab, k], pz[k - 1]) for k in range(1, nz)]
            )
        yield
        s4 = []
        for ab in both:
            i, j = ij[ab]
            total = own[ab, i, j, z].astype(jnp.float32)
            for k in range(1, nz):
                s3[ab][k - 1].wait_recv()
                total = total + r3[ab, k].astype(jnp.float32)
            full[core, ab, i, j, z] = total.astype(jnp.bfloat16)
            piece = full.at[core, ab, i, j, z]
            s4.append([push(piece, piece, pz[k - 1]) for k in range(1, nz)])
        yield
        s5 = []
        for ab in both:
            i, j = ij[ab]
            for copy in s4[ab]:
                copy.wait_recv()
            piece = full.at[core, ab, i, j]
            s5.append(push(piece, piece, pj[ab]))
        yield
        s6, last = [], []
        for ab in both:
            i, j = ij[ab]
            s5[ab].wait_recv()
            piece = full.at[core, ab, i]
            s6.append(push(piece, piece, pi[ab]))
            last.append(push(piece, piece, pc))
        yield
        for ab in both:
            i, j = ij[ab]
            s6[ab].wait_recv()
            piece = full.at[core, ab, 1 - i]
            last.append(push(piece, piece, pc))
        widen(core, full, result, first_column, False)
        yield
        for copy in last:
            copy.wait_recv()
        widen(1 - core, full, result, first_column, False)
        yield

    def back(head, c):
        rows = pl.ds(c * chunk, chunk)
        sums[head, c].wait_recv()
        if head == "t":
            back_t[rows, :] = mm(added(pre_t[rows, :], got_pre_t[rows, :]), wt[...], NT)
        else:
            back_i[rows, :] = mm(added(pre_i[rows, :], got_pre_i[rows, :]), wi[...], NT)

    chains = {}
    for head, kinds, flipped, pre, result, parts in (
        ("t", KINDS_T, xtt, pre_t, ht, bufs_t),
        ("i", KINDS_I, xit, pre_i, hi, bufs_i),
    ):
        for k, kind in enumerate(kinds):
            reduce = reduce_z_first if kind == "z" else reduce_head
            chains[head, k] = reduce(flipped, pre, result, k * (e // len(kinds)), parts[k])
    for what, head, k in ORDER:
        if what == "near":
            texts_of_neighbour(k)
        elif what == "own":
            own_texts()
        elif what == "send":
            send_sum(head, k)
        elif what == "back":
            back(head, k)
        else:
            next(chains[head, k])
    for copy in started:
        copy.wait_send()


def tail(bi, bt, hi, ht, bi_out, bt_out, hi_out, ht_out, sems):
    copies = [
        pltpu.make_async_copy(src, dst, sems.at[k])
        for k, (src, dst) in enumerate(
            ((bi, bi_out), (bt, bt_out), (hi, hi_out), (ht, ht_out))
        )
    ]
    for copy in copies:
        copy.start()
    for copy in copies:
        copy.wait()


def kernel_shards(nz, image_feats, text_feats, image_head, text_head, image_lse, text_lse):
    n, di = image_feats.shape[1:]
    dt, e = text_head.shape
    chunk = n // 4
    bf, f32 = jnp.bfloat16, jnp.float32
    vm = pltpu.VMEM

    def buffers(rows, kinds):
        piece = (rows // (8 * nz), e // len(kinds) // 2)
        x_first = [(2, 2, 2, nz)] * 3 + [(2, 2, nz), (2, nz), (2, nz), (2, 2, 2, 2, nz)]
        z_first = [(nz, 2, 2, 2)] * 4 + [(2, 2), (2,), (2, nz, 2, 2, 2)]
        return [
            [vm((*lead, *piece), bf) for lead in (z_first if kind == "z" else x_first)]
            for kind in kinds
        ]

    copies = 2 + 4 * (n // chunk) + len(KINDS_I + KINDS_T) * (4 + 2 + 2 + 2 * (nz - 1) * 2 + 2 + 2 + 4)
    spec = pl.BlockSpec(memory_space=pltpu.VMEM)
    anywhere = pl.BlockSpec(memory_space=pl.ANY)
    image_back, text_back, image_total, text_total = pl.pallas_call(
        functools.partial(fused, nz, chunk),
        out_shape=[vm((n, di), f32), vm((n, dt), f32), vm((di, e), f32), vm((dt, e), f32)],
        in_specs=[anywhere] * 4 + [spec] * 2,
        out_specs=[spec] * 4,
        scratch_shapes=[
            vm((n, di), bf), vm((n, dt), bf), vm((n, di), bf), vm((n, dt), bf),
            vm((di, e), bf), vm((dt, e), bf),
            vm((2 * n, e), bf), vm((2 * n, e), bf), vm((n, e), bf), vm((n, e), bf),
            vm((n, e), f32), vm((n, e), f32), vm((n, e), f32), vm((n, e), f32),
            vm((n, 1), f32), vm((n, 1), f32), vm((n, 1), f32), vm((n, 1), f32),
            vm((n, e), bf), vm((n, e), bf), vm((n, e), bf), vm((n, e), bf),
            vm((1, n), f32), vm((1, n), f32), vm((2, n, 128), f32), vm((2, 1, n), f32),
            vm((2, 2, n, n), bf),
            vm((n, e), f32), vm((n, e), f32), vm((n, e), f32),
            vm((di, 2 * n), bf), vm((dt, 2 * n), bf),
            buffers(di, KINDS_I), buffers(dt, KINDS_T),
            pltpu.SemaphoreType.DMA((copies,)), pltpu.SemaphoreType.DMA((copies,)),
            pltpu.SemaphoreType.DMA((4,)),
        ],
        compiler_params=pltpu.CompilerParams(
            collective_id=0, has_side_effects=True, vmem_limit_bytes=54 * 1024 * 1024
        ),
    )(image_feats[0], text_feats[0], image_head, text_head, image_lse, text_lse)
    shapes = [(n, di), (n, dt), (di, e), (dt, e)]
    image_back, text_back, image_total, text_total = pl.pallas_call(
        tail,
        out_shape=[jax.ShapeDtypeStruct(shape, f32) for shape in shapes],
        in_specs=[spec] * 4,
        out_specs=[anywhere] * 4,
        scratch_shapes=[pltpu.SemaphoreType.DMA((4,))],
        compiler_params=pltpu.CompilerParams(vmem_limit_bytes=4 * 1024 * 1024),
    )(image_back, text_back, image_total, text_total)
    return (image_back[None], text_back[None], image_total, text_total)


def solution(mesh):
    blk, rep = mesh.shape["blk"], mesh.shape["rep"]
    body = shards
    if blk == SIDE * SIDE and rep % SIDE == 0:
        body = functools.partial(kernel_shards, rep // SIDE)
    return jax.shard_map(
        body,
        mesh=mesh,
        in_specs=(
            P("rep", "blk", None),
            P("rep", "blk", None),
            P(),
            P(),
            P("rep", "blk"),
            P("rep", "blk"),
        ),
        out_specs=(P("rep", "blk", None), P("rep", "blk", None), P(), P()),
        check_vma=False,
    )
```
